32 devices in a mesh: seq: 8 (over z, y), dp: 4 (over x, core).
Axes of the slice: x: 2, y: 2, z: 4, core: 2. Of those that a mesh axis runs over, the one named last changes fastest.
Arguments:
- queries: bfloat16 [1024, 8192], P('seq', 'dp'), may hold values from -6 to 6
- keys: bfloat16 [1024, 8192], P('seq', 'dp'), may hold values from -0.59765625 to 0.59765625
- values: bfloat16 [1024, 8192], P('seq', 'dp'), may hold values from -6 to 6
- output_gradient: bfloat16 [1024, 8192], P('seq', 'dp'), may hold values from -6 to 6
- log_decay: float32 [64, 1024], P('dp', 'seq'), may hold values from -1 to 0, as said below
- gain: float32 [8192], P('dp'), may hold values from 0.1 to 1.9
Outputs:
- query_grad: bfloat16 [1024, 8192], P('seq', 'dp')
- key_grad: bfloat16 [1024, 8192], P('seq', 'dp')
- value_grad: bfloat16 [1024, 8192], P('seq', 'dp')
- gain_grad: float32 [8192], P('dp')
The draws below stay inside these ranges and needn't reach their ends.
Inputs may be any that keep to these rules, and one draw needn't show every extreme that they name: `log_decay`: negative at every token and head.
All inputs are finite; a program needn't handle non-finite values.
Results may differ from the reference program's by a relative error of at most 0.005.
Values sent between devices are 32-bit elements; how exact they have to be, the bound alone decides.
No kernel may reach another device: no remote copies, remote signals or barrier semaphores. Data moves between devices by JAX's collectives and lax.ppermute only.
A program may use at most 128 MiB of HBM per device.

```python
import math
import jax
import jax.numpy as jnp
from jax import lax

H = 64
DH = 128
TOK_DEV = 128
HD = 8192
LENGTH = 1024


def draw_log_decay(key, part):
    keys_all = jax.random.split(key, 7)
    fast_share = 0.4
    picked_items = jax.random.uniform(keys_all[0], (H, 1)) < fast_share
    fast_rate = jnp.exp(jax.random.uniform(keys_all[1], (H, 1), minval=math.log(1.0 / 50.0), maxval=math.log(1.0 / 30.0)))
    slow_rate = jnp.exp(jax.random.uniform(keys_all[2], (H, 1), minval=math.log(0.01 / LENGTH), maxval=math.log(0.1 / LENGTH)))
    base_rate = jnp.where(picked_items, fast_rate, slow_rate)
    block_count = LENGTH // TOK_DEV
    block_factor = jnp.exp(jax.random.uniform(keys_all[3], (H, block_count, 1), minval=-math.log(2.0), maxval=math.log(2.0)))
    block_factor = jnp.broadcast_to(block_factor, (H, block_count, TOK_DEV)).reshape(H, LENGTH)
    token_factor = jax.random.uniform(keys_all[4], (H, LENGTH), minval=0.5, maxval=1.5)
    forgetting_speed = base_rate * block_factor * token_factor
    sequence_indices = jax.random.randint(keys_all[5], (3,), 0, LENGTH)
    objective_numbers = jax.random.uniform(keys_all[6], (3,), minval=0.2, maxval=0.4)
    device_assignment = jnp.arange(LENGTH)
    segment_lengths = jnp.sum(jnp.where(device_assignment[None, :] == sequence_indices[:, None], jnp.log(1.0 - objective_numbers)[:, None], 0.0), axis=0)
    return (-forgetting_speed + segment_lengths[None, :]).astype(jnp.float32)


def block_scale(rng, shape, cuts, smallest, high):
    def one(axis_at, shards_of):
        draws = jax.random.uniform(jax.random.fold_in(jax.random.fold_in(rng, 6), axis_at), (shards_of,), jnp.float32, smallest / len(cuts), high / len(cuts))
        return jnp.repeat(jnp.exp(draws), shape[axis_at] // shards_of).reshape((-1,) + (1,) * (len(shape) - axis_at - 1))

    loudness = one(*cuts[0])
    for cut in cuts[1:]:
        loudness = loudness * one(*cut)
    return loudness


def scatter_about(stream_key, shape, width, bound, cuts=(), kind=jnp.bfloat16):
    drawn = jax.random.normal(stream_key, shape, jnp.float32) * width
    if len(cuts) > 0:
        drawn = block_scale(stream_key, shape, cuts, -0.22, 0.18) * drawn
    return jnp.clip(drawn, min=-bound, max=bound).astype(kind)


def setup_inputs(seed: int = 0) -> dict:
    arg_keys = jax.random.split(jax.random.key(seed), 7)
    return {
        "queries": scatter_about(arg_keys[0], (LENGTH, HD), 1.0, 6.0, ((0, 8), (1, 4))),
        "keys": scatter_about(arg_keys[1], (LENGTH, HD), 0.1, 0.59765625, ((0, 8), (1, 4))),
        "values": scatter_about(arg_keys[2], (LENGTH, HD), 1.0, 6.0, ((0, 8), (1, 4))),
        "output_gradient": scatter_about(arg_keys[3], (LENGTH, HD), 1.0, 6.0, ((0, 8), (1, 4))),
        "log_decay": draw_log_decay(jax.random.fold_in(arg_keys[6], 71), 0),
        "gain": jnp.clip(1.0 + 0.18 * jax.random.normal(arg_keys[5], (HD,), jnp.float32), 0.1, 1.9),
    }


epsilon = 1e-05
highest = lax.Precision.HIGHEST

def block_weights(cum):
    row_index = lax.broadcasted_iota(jnp.int32, (TOK_DEV, TOK_DEV), 0)
    col_index = lax.broadcasted_iota(jnp.int32, (TOK_DEV, TOK_DEV), 1)
    causal_mask = row_index >= col_index
    dispersion_factor = cum[:, :, None] - cum[:, None, :]
    return jnp.where(causal_mask[None], jnp.exp(jnp.minimum(dispersion_factor, 0.0)), 0.0)

def carry_step(state, item):
    decay_now, local_now = item
    return (decay_now[:, None, None] * state + local_now, state)

def reference(queries, keys, values, output_gradient, log_decay, gain):
    blocks = LENGTH // TOK_DEV
    shape_four = (blocks, TOK_DEV, H, DH)
    query_b = queries.reshape(shape_four)
    key_b = keys.reshape(shape_four)
    value_b = values.reshape(shape_four)
    grad_b = output_gradient.reshape(blocks, TOK_DEV, H * DH)
    cumulative = jnp.cumsum(log_decay.reshape(H, blocks, TOK_DEV), axis=2).transpose(1, 0, 2)
    last = cumulative[:, :, -1]
    total_decay = jnp.exp(last)

    def state_of(packed):
        key_now, value_now, cum, lst = packed
        tail_t = jnp.exp(lst[:, None] - cum).T[..., None]
        return jnp.einsum('thd,the->hde', key_now.astype(jnp.float32) * tail_t, value_now.astype(jnp.float32), precision=highest)
    local_state = lax.map(state_of, (key_b, value_b, cumulative, last))
    start_state = jnp.zeros((H, DH, DH), jnp.float32)
    _, incoming = lax.scan(carry_step, start_state, (total_decay, local_state))

    def forward_of(packed):
        query_now, key_now, value_now, grad_now, cum, inc = packed
        query_f = query_now.astype(jnp.float32)
        key_f = key_now.astype(jnp.float32)
        value_f = value_now.astype(jnp.float32)
        weights = block_weights(cum)
        lead_t = jnp.exp(cum).T[..., None]
        similarity_matrix = jnp.einsum('thd,shd->hts', query_f, key_f, precision=highest)
        mixed_b = (similarity_matrix * weights).astype(jnp.bfloat16)
        mixed_f = lax.optimization_barrier(mixed_b).astype(jnp.float32)
        inner = jnp.einsum('hts,shd->thd', mixed_f, value_f, precision=highest)
        outer = jnp.einsum('thd,hde->the', query_f, inc, precision=highest) * lead_t
        attn = (inner + outer).reshape(TOK_DEV, H * DH)
        inv_rms = lax.rsqrt(lax.optimization_barrier(jnp.mean(attn * attn, axis=-1, keepdims=True)) + epsilon)
        normed = attn * inv_rms
        grad_f = grad_now.astype(jnp.float32)
        multiplied_entries = grad_f * gain
        d_attn = (inv_rms * (multiplied_entries - normed * lax.optimization_barrier(jnp.mean(multiplied_entries * normed, axis=-1, keepdims=True)))).astype(jnp.bfloat16)
        gain_part = lax.optimization_barrier(jnp.sum(grad_f * normed, axis=0))
        d_attn_f = lax.optimization_barrier(d_attn).astype(jnp.float32).reshape(TOK_DEV, H, DH)
        local_back = jnp.einsum('thd,the->hde', query_f * lead_t, d_attn_f, precision=highest)
        return (d_attn, gain_part, local_back)
    d_attn_all, gain_parts, local_back = lax.map(forward_of, (query_b, key_b, value_b, grad_b, cumulative, incoming))
    _, later = lax.scan(carry_step, start_state, (total_decay, local_back), reverse=True)

    def grads_of(packed):
        query_now, key_now, value_now, d_now, cum, lst, inc, lat = packed
        query_f = query_now.astype(jnp.float32)
        key_f = key_now.astype(jnp.float32)
        value_f = value_now.astype(jnp.float32)
        d_attn_f = d_now.astype(jnp.float32).reshape(TOK_DEV, H, DH)
        weights = block_weights(cum)
        lead_t = jnp.exp(cum).T[..., None]
        tail_t = jnp.exp(lst[:, None] - cum).T[..., None]
        similarity_matrix = jnp.einsum('thd,shd->hts', query_f, key_f, precision=highest)
        mixed_b = (similarity_matrix * weights).astype(jnp.bfloat16)
        mixed_f = lax.optimization_barrier(mixed_b).astype(jnp.float32)
        dprod = jnp.einsum('thd,shd->hts', d_attn_f, value_f, precision=highest)
        graded_b = (dprod * weights).astype(jnp.bfloat16)
        graded_f = lax.optimization_barrier(graded_b).astype(jnp.float32)
        query_grad = jnp.einsum('hts,shd->thd', graded_f, key_f, precision=highest)
        query_grad = query_grad + jnp.einsum('the,hde->thd', d_attn_f, inc, precision=highest) * lead_t
        key_grad = jnp.einsum('hts,thd->shd', graded_f, query_f, precision=highest)
        key_grad = key_grad + jnp.einsum('the,hde->thd', value_f, lat, precision=highest) * tail_t
        value_grad = jnp.einsum('hts,thd->shd', mixed_f, d_attn_f, precision=highest)
        value_grad = value_grad + jnp.einsum('thd,hde->the', key_f, lat, precision=highest) * tail_t
        return (query_grad.reshape(TOK_DEV, H * DH).astype(jnp.bfloat16), key_grad.reshape(TOK_DEV, H * DH).astype(jnp.bfloat16), value_grad.reshape(TOK_DEV, H * DH).astype(jnp.bfloat16))
    query_grad, key_grad, value_grad = lax.map(grads_of, (query_b, key_b, value_b, d_attn_all, cumulative, last, incoming, later))
    return (query_grad.reshape(LENGTH, H * DH), key_grad.reshape(LENGTH, H * DH), value_grad.reshape(LENGTH, H * DH), lax.optimization_barrier(jnp.sum(gain_parts, axis=0)))
```

```python
import functools

import jax
import jax.numpy as jnp
from jax import lax
from jax.experimental import pallas as pl
from jax.experimental.pallas import tpu as pltpu
from jax.sharding import PartitionSpec as P

epsilon = 1e-05
highest = lax.Precision.HIGHEST
f32 = jnp.float32
bf16 = jnp.bfloat16
VMEM = pl.BlockSpec(memory_space=pltpu.VMEM)
SMEM = pl.BlockSpec(memory_space=pltpu.SMEM)
GRANT = 24 * 2**20


def call(body, outs, flops, moved, name):
    def run(side, *arrays):
        return pl.pallas_call(
            body,
            out_shape=[jax.ShapeDtypeStruct(*o) for o in outs],
            in_specs=[SMEM] + [VMEM] * len(arrays),
            out_specs=[VMEM] * len(outs),
            compiler_params=pltpu.CompilerParams(vmem_limit_bytes=GRANT),
            cost_estimate=pl.CostEstimate(flops=flops, bytes_accessed=moved, transcendentals=0),
            name=name,
        )(side, *arrays)

    return run


def dot(a, b, ca, cb):
    return lax.dot_general(a, b, (((ca,), (cb,)), ((), ())), preferred_element_type=f32)


def split(x):
    hi = x.astype(bf16)
    return hi, (x - hi.astype(f32)).astype(bf16)


def column(table, side, half, j):
    return jnp.where(side == 0, table[:, j : j + 1], table[:, half + j : half + j + 1])


def lanes(side, half, j, dim):
    return pl.ds(pl.multiple_of((side * half + j) * dim, dim), dim)


def tables(ld):
    tok = ld.shape[1]
    row = lax.broadcasted_iota(jnp.int32, (tok, tok), 0)
    col = lax.broadcasted_iota(jnp.int32, (tok, tok), 1)
    lower = (row >= col).astype(f32)
    dims = (((1,), (1,)), ((), ()))
    cum_t = lax.dot_general(lower, ld, dims, precision=highest, preferred_element_type=f32)
    cum_r = lax.dot_general(ld, lower, dims, precision=highest, preferred_element_type=f32)
    return cum_t, cum_r


def state_into(outs, a_ref, b_of, factor, side, half, dim):
    j = 0
    for out in outs:
        for i in range(out.shape[0]):
            hi, lo = split(a_ref[:, lanes(side, half, j, dim)].astype(f32) * column(factor, side, half, j))
            b = b_of(j)
            out[i] = dot(hi, b, 0, 0) + dot(lo, b, 0, 0)
            j += 1


def first_states(half, dim, side_ref, k_ref, v_ref, ld_ref, cum_t_ref, cum_r_ref, total_ref, *outs):
    side = side_ref[0]
    cum_t, cum_r = tables(ld_ref[...])
    cum_t_ref[...] = cum_t
    cum_r_ref[...] = cum_r
    tok = cum_t.shape[0]
    total_ref[...] = jnp.broadcast_to(jnp.exp(cum_r[:, tok - 1 :]), total_ref.shape)
    tail = jnp.exp(cum_t[tok - 1 :, :] - cum_t)
    state_into(outs, k_ref, lambda j: v_ref[:, lanes(side, half, j, dim)], tail, side, half, dim)


def more_states(half, dim, side_ref, k_ref, v_ref, cum_t_ref, *outs):
    side = side_ref[0]
    cum_t = cum_t_ref[...]
    tail = jnp.exp(cum_t[cum_t.shape[0] - 1 :, :] - cum_t)
    state_into(outs, k_ref, lambda j: v_ref[:, lanes(side, half, j, dim)], tail, side, half, dim)


def weights_of(cum_t, cum_r, h):
    tok = cum_t.shape[0]
    row = lax.broadcasted_iota(jnp.int32, (tok, tok), 0)
    col = lax.broadcasted_iota(jnp.int32, (tok, tok), 1)
    gap = cum_t[:, h : h + 1] - cum_r[h : h + 1, :]
    return jnp.where(row >= col, jnp.exp(jnp.minimum(gap, 0.0)), 0.0)


def within(heads, dim, side_ref, q_ref, k_ref, v_ref, cum_t_ref, cum_r_ref, mixed_ref, inner_ref):
    cum_t, cum_r = cum_t_ref[...], cum_r_ref[...]
    for h in range(heads):
        at = slice(h * dim, (h + 1) * dim)
        scores = dot(q_ref[:, at], k_ref[:, at], 1, 1)
        mixed = (scores * weights_of(cum_t, cum_r, h)).astype(bf16)
        mixed_ref[h] = mixed
        inner_ref[:, at] = dot(mixed, v_ref[:, at], 1, 0)


def across(half, dim, start, count, have, last, side_ref, *refs):
    side = side_ref[0]
    q_ref, inner_ref, g_ref, gain_ref, cum_t_ref = refs[:5]
    before = refs[5 : 5 + have]
    states = refs[5 + have : -2]
    attn_ref, sums_ref = refs[-2:]
    lead = jnp.exp(cum_t_ref[...])
    squares = cross = jnp.zeros((lead.shape[0], dim), f32)
    j = start
    for ref in states:
        for i in range(ref.shape[0]):
            at = lanes(side, half, j, dim)
            hi, lo = split(ref[i])
            q = q_ref[:, at]
            outer = (dot(q, hi, 1, 0) + dot(q, lo, 1, 0)) * column(lead, side, half, j)
            attn = inner_ref[:, at] + outer
            attn_ref[:, (j - start) * dim : (j - start + 1) * dim] = attn
            scaled = g_ref[:, at].astype(f32) * gain_ref[:, at]
            squares += attn * attn
            cross += scaled * attn
            j += 1
    for ref in before:
        squares += ref[0]
        cross += ref[1]
    if last:
        sums_ref[0:1, :] = jnp.sum(squares.T, axis=0, keepdims=True)
        sums_ref[1:2, :] = jnp.sum(cross.T, axis=0, keepdims=True)
        sums_ref[2:, :] = jnp.zeros((sums_ref.shape[0] - 2, sums_ref.shape[1]), f32)
    else:
        sums_ref[0] = squares
        sums_ref[1] = cross


def gradient(half, dim, full_width, n_sums, n_attn, side_ref, *refs):
    side = side_ref[0]
    q_ref, g_ref, gain_ref, cum_t_ref = refs[:4]
    sums = refs[4 : 4 + n_sums]
    attns = refs[4 + n_sums : 4 + n_sums + n_attn]
    d_ref, gain_part_ref = refs[4 + n_sums + n_attn :][:2]
    outs = refs[4 + n_sums + n_attn + 2 :]
    total = sums[0][...]
    for ref in sums[1:]:
        total = total + ref[...]
    inv_row = lax.rsqrt(total[0:1] / full_width + epsilon)
    mean_row = inv_row * (total[1:2] / full_width)
    tok = inv_row.shape[1]
    inv = jnp.broadcast_to(inv_row, (tok, tok)).T
    mean = jnp.broadcast_to(mean_row, (tok, tok)).T
    lead = jnp.exp(cum_t_ref[...])
    kept = {}
    j = 0
    for ref in attns:
        for i in range(ref.shape[1] // dim):
            at = lanes(side, half, j, dim)
            normed = ref[:, i * dim : (i + 1) * dim] * inv
            g = g_ref[:, at].astype(f32)
            d = (inv * (g * gain_ref[:, at] - normed * mean)).astype(bf16)
            d_ref[:, j * dim : (j + 1) * dim] = d
            gain_part_ref[j : j + 1, :] = jnp.sum(g * normed, axis=0, keepdims=True)
            kept[j] = d
            j += 1
    state_into(outs, q_ref, lambda j: kept[j], lead, side, half, dim)


def local_grads(half, dim, chunks, side_ref, *refs):
    side = side_ref[0]
    q_ref, k_ref, v_ref, cum_t_ref, cum_r_ref, mixed_ref, d_own_ref, d_give_ref = refs[:8]
    states = refs[8 : 8 + 2 * chunks]
    qg_ref, kg_ref, vg_ref = refs[8 + 2 * chunks :]
    cum_t = cum_t_ref[...]
    lead = jnp.exp(cum_t)
    tok = cum_t.shape[0]
    row = lax.broadcasted_iota(jnp.int32, (tok, tok), 0)
    col = lax.broadcasted_iota(jnp.int32, (tok, tok), 1)
    for s, (d_ref, group) in enumerate(((d_own_ref, states[:chunks]), (d_give_ref, states[chunks:]))):
        which = side if s == 0 else 1 - side
        j = 0
        for ref in group:
            for i in range(ref.shape[0]):
                at = lanes(which, half, j, dim)
                h = which * half + j
                d = d_ref[:, j * dim : (j + 1) * dim]
                cum_col = column(cum_t, which, half, j)
                gap = cum_col - cum_r_ref[pl.ds(h, 1), :]
                weights = jnp.where(row >= col, jnp.exp(jnp.minimum(gap, 0.0)), 0.0)
                graded = (dot(d, v_ref[:, at], 1, 1) * weights).astype(bf16)
                hi, lo = split(ref[i])
                outer = (dot(d, hi, 1, 1) + dot(d, lo, 1, 1)) * column(lead, which, half, j)
                qg_ref[:, at] = (dot(graded, k_ref[:, at], 1, 0) + outer).astype(bf16)
                kg_ref[:, at] = dot(graded, q_ref[:, at], 0, 0)
                vg_ref[:, at] = dot(mixed_ref[h], d, 0, 0)
                j += 1


def final_grads(half, dim, chunks, side_ref, *refs):
    side = side_ref[0]
    k_ref, v_ref, cum_t_ref, kg_ref, vg_ref = refs[:5]
    states = refs[5 : 5 + 2 * chunks]
    key_ref, value_ref = refs[5 + 2 * chunks :]
    cum_t = cum_t_ref[...]
    tail = jnp.exp(cum_t[cum_t.shape[0] - 1 :, :] - cum_t)
    for s, group in enumerate((states[:chunks], states[chunks:])):
        which = side if s == 0 else 1 - side
        j = 0
        for ref in group:
            for i in range(ref.shape[0]):
                at = lanes(which, half, j, dim)
                tail_col = column(tail, which, half, j)
                hi, lo = split(ref[i])
                v, k = v_ref[:, at], k_ref[:, at]
                key_ref[:, at] = (kg_ref[:, at] + (dot(v, hi, 1, 1) + dot(v, lo, 1, 1)) * tail_col).astype(bf16)
                value_ref[:, at] = (vg_ref[:, at] + (dot(k, hi, 1, 0) + dot(k, lo, 1, 0)) * tail_col).astype(bf16)
                j += 1


def carried(mine, theirs, total_mine, total_theirs, place, n_seq, n_dp, reverse):
    pairs = n_seq // 2
    block = n_seq - 1 - place if reverse else place
    first = block % 2 == 0
    pair = block // 2
    swap = [(i, i ^ 1) for i in range(n_seq)]

    def hop(a):
        b = a + 1
        lo, hi = (pairs - 1 - a, pairs - 1 - b) if reverse else (a, b)
        perm = []
        for s in range(n_seq):
            for d in range(n_dp):
                if s // 2 == lo:
                    to = (s + 2 * (hi - lo)) * n_dp + d
                elif s // 2 == hi:
                    to = (s - 2 * (hi - lo)) * n_dp + d
                else:
                    to = s * n_dp + (d ^ 1)
                perm.append((s * n_dp + d, to))
        return perm

    received = [lax.ppermute(x, "seq", swap) for x in theirs]
    kept, sent = [], []
    at = 0
    cuts = []
    for x in mine:
        n = x.shape[0]
        cuts.append((total_mine[at : at + n, None, :], total_theirs[at : at + n, None, :]))
        at += n
    sums = [
        jnp.where(first, their_decay, 1.0) * x + jnp.where(first, 1.0, my_decay) * r
        for x, r, (my_decay, their_decay) in zip(mine, received, cuts)
    ]
    both = [a * b for a, b in cuts]
    inward = [None] * len(mine)
    outward = sums
    for a in range(pairs - 1):
        got = [lax.ppermute(x, ("seq", "dp"), hop(a)) for x in outward]
        here = pair == a + 1
        inward = [
            jnp.where(here, g, 0.0 if e is None else e) for g, e in zip(got, inward)
        ]
        outward = [s + d * g for s, d, g in zip(sums, both, got)]
    for x, r, e, (my_decay, their_decay) in zip(mine, received, inward, cuts):
        if e is None:
            e = jnp.zeros_like(x)
        through = jnp.where(first, my_decay, their_decay) * e + jnp.where(first, x, r)
        kept.append(jnp.where(first, e, through))
        sent.append(jnp.where(first, through, e))
    return kept, [lax.ppermute(x, "seq", swap) for x in sent]


def on_device(n_seq, n_dp, queries, keys, values, output_gradient, log_decay, gain):
    tok, width = queries.shape
    heads = log_decay.shape[0]
    dim = width // heads
    half = heads // 2
    chunks = min(4, half)
    sizes = [half // chunks + (1 if i < half % chunks else 0) for i in range(chunks)]
    full_width = width * n_dp
    place = lax.axis_index("seq")
    own = (place % 2).astype(jnp.int32)
    own_side = own.reshape(1)
    give_side = (1 - own).reshape(1)
    gain_row = gain.reshape(1, width)
    pair_flops = 2 * tok * dim * dim
    state = [((n, dim, dim), f32) for n in sizes]
    row_bytes = tok * half * dim

    cum_t, cum_r, total, *give = call(
        functools.partial(first_states, half, dim),
        [((tok, heads), f32), ((heads, tok), f32), ((heads, dim), f32)] + state,
        2 * half * pair_flops, 8 * row_bytes, "first_states",
    )(give_side, keys, values, log_decay)
    swap = [(i, i ^ 1) for i in range(n_seq)]
    other = lax.ppermute(total, "seq", swap)
    own_states = call(
        functools.partial(more_states, half, dim), state, 2 * half * pair_flops, 8 * row_bytes, "more_states"
    )(own_side, keys, values, cum_t)
    mixed, inner = call(
        functools.partial(within, heads, dim),
        [((heads, tok, tok), bf16), ((tok, width), f32)],
        2 * heads * pair_flops, 12 * row_bytes, "within",
    )(own_side, queries, keys, values, cum_t, cum_r)

    upper = own == 1
    total_mine = jnp.where(upper, total[half:], total[:half])
    total_theirs = jnp.where(upper, other[half:], other[:half])
    in_own, in_give = carried(own_states, give, total_mine, total_theirs, place, n_seq, n_dp, False)

    def outer(side, states, start, before, last, name):
        count = sum(x.shape[0] for x in states)
        return call(
            functools.partial(across, half, dim, start, count, len(before), last),
            [((tok, count * dim), f32), ((8, tok), f32) if last else ((2, tok, dim), f32)],
            2 * count * pair_flops, 14 * tok * count * dim, name,
        )(side, queries, inner, output_gradient, gain_row, cum_t, *before, *states)

    attn_own, part = outer(own_side, in_own, 0, [], False, "across_own")
    early = sum(sizes[:-1])
    if early:
        attn_early, more = outer(give_side, in_give[:-1], 0, [part], False, "across_early")
        attn_late, sums = outer(give_side, in_give[-1:], early, [more], True, "across_late")
        attn_give = [attn_early, attn_late]
    else:
        attn_late, sums = outer(give_side, in_give, 0, [part], True, "across_late")
        attn_give = [attn_late]

    if n_dp <= 4:
        all_sums = [sums] + [
            lax.ppermute(sums, "dp", [(i, i ^ m) for i in range(n_dp)]) for m in range(1, n_dp)
        ]
    else:
        all_sums = [lax.psum(sums, "dp")]

    def grads(side, attns, name):
        return call(
            functools.partial(gradient, half, dim, full_width, len(all_sums), len(attns)),
            [((tok, half * dim), bf16), ((half, dim), f32)] + state,
            2 * half * pair_flops, 14 * row_bytes, name,
        )(side, queries, output_gradient, gain_row, cum_t, *all_sums, *attns)

    d_give, gain_give, *back_give = grads(give_side, attn_give, "gradient_give")
    d_own, gain_own, *back_own = grads(own_side, [attn_own], "gradient_own")
    query_grad, key_part, value_part = call(
        functools.partial(local_grads, half, dim, chunks),
        [((tok, width), bf16), ((tok, width), f32), ((tok, width), f32)],
        6 * heads * pair_flops, 40 * row_bytes, "local_grads",
    )(own_side, queries, keys, values, cum_t, cum_r, mixed, d_own, d_give, *in_own, *in_give)

    late_own, late_give = carried(back_own, back_give, total_mine, total_theirs, place, n_seq, n_dp, True)

    gain_grad = jnp.concatenate(
        [jnp.where(upper, gain_give, gain_own), jnp.where(upper, gain_own, gain_give)], axis=0
    )
    step = 1
    while step < n_seq:
        gain_grad = gain_grad + lax.ppermute(gain_grad, "seq", [(i, i ^ step) for i in range(n_seq)])
        step *= 2

    key_grad, value_grad = call(
        functools.partial(final_grads, half, dim, chunks),
        [((tok, width), bf16), ((tok, width), bf16)],
        4 * heads * pair_flops, 32 * row_bytes, "final_grads",
    )(own_side, keys, values, cum_t, key_part, value_part, *late_own, *late_give)
    return query_grad, key_grad, value_grad, gain_grad.reshape(width)


def solution(mesh):
    return jax.shard_map(
        functools.partial(on_device, mesh.shape["seq"], mesh.shape["dp"]),
        mesh=mesh,
        in_specs=(P("seq", "dp"), P("seq", "dp"), P("seq", "dp"), P("seq", "dp"), P("dp", "seq"), P("dp")),
        out_specs=(P("seq", "dp"), P("seq", "dp"), P("seq", "dp"), P("dp")),
        check_vma=False,
    )
```

```python
import functools

import jax
import jax.numpy as jnp
from jax import lax
from jax.experimental import pallas as pl
from jax.experimental.pallas import tpu as pltpu
from jax.sharding import PartitionSpec as P


epsilon = 1e-05
highest = lax.Precision.HIGHEST
f32 = jnp.float32
bf16 = jnp.bfloat16
VMEM = pl.BlockSpec(memory_space=pltpu.VMEM)
SMEM = pl.BlockSpec(memory_space=pltpu.SMEM)
GRANT = 24 * 2**20


def call(body, outs, flops, moved):
    def run(place, *arrays):
        return pl.pallas_call(
            body,
            out_shape=[jax.ShapeDtypeStruct(*o) for o in outs],
            in_specs=[SMEM] + [VMEM] * len(arrays),
            out_specs=[VMEM] * len(outs),
            compiler_params=pltpu.CompilerParams(vmem_limit_bytes=GRANT),
            cost_estimate=pl.CostEstimate(flops=flops, bytes_accessed=moved, transcendentals=0),
        )(place, *arrays)

    return run


def dot(a, b, ca, cb):
    return lax.dot_general(a, b, (((ca,), (cb,)), ((), ())), preferred_element_type=f32)


def split(x):
    hi = x.astype(bf16)
    return hi, (x - hi.astype(f32)).astype(bf16)


def column(table, side, half, j):
    return jnp.where(side == 0, table[:, j : j + 1], table[:, half + j : half + j + 1])


def side_of(place_ref, give):
    own = place_ref[0] & 1
    return 1 - own if give else own


def flags_of(place, pairs, shape):
    row = lax.broadcasted_iota(jnp.int32, shape, 0)
    odd, pair = place & 1, place >> 1
    forward = (row >= 3) & (row < 2 + pairs) & (row - 2 == pair)
    reverse = (row >= 2 + pairs) & (row < 1 + 2 * pairs) & (row - 1 - pairs == pairs - 1 - pair)
    even = jnp.full(shape, odd, jnp.int32) == 0
    on = ((row == 0) & ~even) | ((row == 1) & even) | ((row == 2) & ~even) | forward | reverse
    return on.astype(f32)


def lanes(side, half, j, dim):
    return pl.ds(pl.multiple_of((side * half + j) * dim, dim), dim)


def tables(ld):
    tok = ld.shape[1]
    row = lax.broadcasted_iota(jnp.int32, (tok, tok), 0)
    col = lax.broadcasted_iota(jnp.int32, (tok, tok), 1)
    lower = (row >= col).astype(f32)
    dims = (((1,), (1,)), ((), ()))
    cum_t = lax.dot_general(lower, ld, dims, precision=highest, preferred_element_type=f32)
    cum_r = lax.dot_general(ld, lower, dims, precision=highest, preferred_element_type=f32)
    return cum_t, cum_r


def state_into(outs, a_ref, b_of, factor, side, half, dim):
    j = 0
    for out in outs:
        for i in range(out.shape[0]):
            hi, lo = split(a_ref[:, lanes(side, half, j, dim)].astype(f32) * column(factor, side, half, j))
            b = b_of(j)
            out[i] = dot(hi, b, 0, 0) + dot(lo, b, 0, 0)
            j += 1


def first_states(half, dim, pairs, place_ref, k_ref, v_ref, ld_ref, cum_t_ref, cum_r_ref, total_ref, flags_ref, *outs):
    side = side_of(place_ref, True)
    flags_ref[...] = flags_of(place_ref[0], pairs, flags_ref.shape)
    cum_t, cum_r = tables(ld_ref[...])
    cum_t_ref[...] = cum_t
    cum_r_ref[...] = cum_r
    tok = cum_t.shape[0]
    total_ref[...] = jnp.broadcast_to(jnp.exp(cum_r[:, tok - 1 :]), total_ref.shape)
    tail = jnp.exp(cum_t[tok - 1 :, :] - cum_t)
    state_into(outs, k_ref, lambda j: v_ref[:, lanes(side, half, j, dim)], tail, side, half, dim)


def more_states(half, dim, place_ref, k_ref, v_ref, cum_t_ref, *outs):
    side = side_of(place_ref, False)
    cum_t = cum_t_ref[...]
    tail = jnp.exp(cum_t[cum_t.shape[0] - 1 :, :] - cum_t)
    state_into(outs, k_ref, lambda j: v_ref[:, lanes(side, half, j, dim)], tail, side, half, dim)


def weights_of(cum_t, cum_r, h):
    tok = cum_t.shape[0]
    row = lax.broadcasted_iota(jnp.int32, (tok, tok), 0)
    col = lax.broadcasted_iota(jnp.int32, (tok, tok), 1)
    gap = cum_t[:, h : h + 1] - cum_r[h : h + 1, :]
    return jnp.where(row >= col, jnp.exp(jnp.minimum(gap, 0.0)), 0.0)


def within(heads, dim, place_ref, q_ref, k_ref, v_ref, cum_t_ref, cum_r_ref, mixed_ref, inner_ref):
    cum_t, cum_r = cum_t_ref[...], cum_r_ref[...]
    for h in range(heads):
        at = slice(h * dim, (h + 1) * dim)
        scores = dot(q_ref[:, at], k_ref[:, at], 1, 1)
        mixed = (scores * weights_of(cum_t, cum_r, h)).astype(bf16)
        mixed_ref[h] = mixed
        inner_ref[:, at] = dot(mixed, v_ref[:, at], 1, 0)


def across(half, dim, give, start, have, last, place_ref, *refs):
    side = side_of(place_ref, give)
    q_ref, inner_ref, g_ref, gain_ref, cum_t_ref = refs[:5]
    before = refs[5 : 5 + have]
    states = refs[5 + have : -2]
    attn_ref, sums_ref = refs[-2:]
    lead = jnp.exp(cum_t_ref[...])
    squares = cross = jnp.zeros((lead.shape[0], dim), f32)
    j = start
    for ref in states:
        for i in range(ref.shape[0]):
            at = lanes(side, half, j, dim)
            hi, lo = split(ref[i])
            q = q_ref[:, at]
            outer = (dot(q, hi, 1, 0) + dot(q, lo, 1, 0)) * column(lead, side, half, j)
            attn = inner_ref[:, at] + outer
            attn_ref[:, (j - start) * dim : (j - start + 1) * dim] = attn
            scaled = g_ref[:, at].astype(f32) * gain_ref[:, at]
            squares += attn * attn
            cross += scaled * attn
            j += 1
    for ref in before:
        squares += ref[0]
        cross += ref[1]
    if last:
        sums_ref[0:1, :] = jnp.sum(squares.T, axis=0, keepdims=True)
        sums_ref[1:2, :] = jnp.sum(cross.T, axis=0, keepdims=True)
        sums_ref[2:, :] = jnp.zeros((sums_ref.shape[0] - 2, sums_ref.shape[1]), f32)
    else:
        sums_ref[0] = squares
        sums_ref[1] = cross


def gradient(half, dim, give, full_width, n_sums, n_attn, place_ref, *refs):
    side = side_of(place_ref, give)
    q_ref, g_ref, gain_ref, cum_t_ref = refs[:4]
    sums = refs[4 : 4 + n_sums]
    attns = refs[4 + n_sums : 4 + n_sums + n_attn]
    d_ref, gain_part_ref = refs[4 + n_sums + n_attn :][:2]
    outs = refs[4 + n_sums + n_attn + 2 :]
    total = sums[0][...]
    for ref in sums[1:]:
        total = total + ref[...]
    inv_row = lax.rsqrt(total[0:1] / full_width + epsilon)
    mean_row = inv_row * (total[1:2] / full_width)
    tok = inv_row.shape[1]
    inv = jnp.broadcast_to(inv_row, (tok, tok)).T
    mean = jnp.broadcast_to(mean_row, (tok, tok)).T
    lead = jnp.exp(cum_t_ref[...])
    kept = {}
    j = 0
    for ref in attns:
        for i in range(ref.shape[1] // dim):
            at = lanes(side, half, j, dim)
            normed = ref[:, i * dim : (i + 1) * dim] * inv
            g = g_ref[:, at].astype(f32)
            d = (inv * (g * gain_ref[:, at] - normed * mean)).astype(bf16)
            d_ref[:, j * dim : (j + 1) * dim] = d
            gain_part_ref[j : j + 1, :] = jnp.sum(g * normed, axis=0, keepdims=True)
            kept[j] = d
            j += 1
    state_into(outs, q_ref, lambda j: kept[j], lead, side, half, dim)


def local_grads(half, dim, chunks, place_ref, *refs):
    side = side_of(place_ref, False)
    q_ref, k_ref, v_ref, cum_t_ref, cum_r_ref, mixed_ref, d_own_ref, d_give_ref = refs[:8]
    states = refs[8 : 8 + 2 * chunks]
    qg_ref, kg_ref, vg_ref = refs[8 + 2 * chunks :]
    cum_t = cum_t_ref[...]
    lead = jnp.exp(cum_t)
    tok = cum_t.shape[0]
    row = lax.broadcasted_iota(jnp.int32, (tok, tok), 0)
    col = lax.broadcasted_iota(jnp.int32, (tok, tok), 1)
    for s, (d_ref, group) in enumerate(((d_own_ref, states[:chunks]), (d_give_ref, states[chunks:]))):
        which = side if s == 0 else 1 - side
        j = 0
        for ref in group:
            for i in range(ref.shape[0]):
                at = lanes(which, half, j, dim)
                h = which * half + j
                d = d_ref[:, j * dim : (j + 1) * dim]
                cum_col = column(cum_t, which, half, j)
                gap = cum_col - cum_r_ref[pl.ds(h, 1), :]
                weights = jnp.where(row >= col, jnp.exp(jnp.minimum(gap, 0.0)), 0.0)
                graded = (dot(d, v_ref[:, at], 1, 1) * weights).astype(bf16)
                hi, lo = split(ref[i])
                outer = (dot(d, hi, 1, 1) + dot(d, lo, 1, 1)) * column(lead, which, half, j)
                qg_ref[:, at] = (dot(graded, k_ref[:, at], 1, 0) + outer).astype(bf16)
                kg_ref[:, at] = dot(graded, q_ref[:, at], 0, 0)
                vg_ref[:, at] = dot(mixed_ref[h], d, 0, 0)
                j += 1


def final_grads(half, dim, chunks, place_ref, *refs):
    side = side_of(place_ref, False)
    k_ref, v_ref, cum_t_ref, kg_ref, vg_ref = refs[:5]
    states = refs[5 : 5 + 2 * chunks]
    key_ref, value_ref = refs[5 + 2 * chunks :]
    cum_t = cum_t_ref[...]
    tail = jnp.exp(cum_t[cum_t.shape[0] - 1 :, :] - cum_t)
    for s, group in enumerate((states[:chunks], states[chunks:])):
        which = side if s == 0 else 1 - side
        j = 0
        for ref in group:
            for i in range(ref.shape[0]):
                at = lanes(which, half, j, dim)
                tail_col = column(tail, which, half, j)
                hi, lo = split(ref[i])
                v, k = v_ref[:, at], k_ref[:, at]
                key_ref[:, at] = (kg_ref[:, at] + (dot(v, hi, 1, 1) + dot(v, lo, 1, 1)) * tail_col).astype(bf16)
                value_ref[:, at] = (vg_ref[:, at] + (dot(k, hi, 1, 0) + dot(k, lo, 1, 0)) * tail_col).astype(bf16)
                j += 1


def carried(mine, theirs, total_mine, total_theirs, flags, n_seq, n_dp, reverse):
    pairs = n_seq // 2
    first = flags[2 if reverse else 1]
    base = 2 + pairs if reverse else 3
    swap = [(i, i ^ 1) for i in range(n_seq)]

    def hop(a):
        b = a + 1
        lo, hi = (pairs - 1 - a, pairs - 1 - b) if reverse else (a, b)
        perm = []
        for s in range(n_seq):
            for d in range(n_dp):
                if s // 2 == lo:
                    to = (s + 2 * (hi - lo)) * n_dp + d
                elif s // 2 == hi:
                    to = (s - 2 * (hi - lo)) * n_dp + d
                else:
                    to = s * n_dp + (d ^ 1)
                perm.append((s * n_dp + d, to))
        return perm

    received = [lax.ppermute(x, "seq", swap) for x in theirs]
    kept, sent = [], []
    at = 0
    cuts = []
    for x in mine:
        n = x.shape[0]
        cuts.append((total_mine[at : at + n, None, :], total_theirs[at : at + n, None, :]))
        at += n
    sums = [
        jnp.where(first > 0.5, their_decay, 1.0) * x + jnp.where(first > 0.5, 1.0, my_decay) * r
        for x, r, (my_decay, their_decay) in zip(mine, received, cuts)
    ]
    both = [a * b for a, b in cuts]
    inward = [None] * len(mine)
    outward = sums
    for a in range(pairs - 1):
        got = [lax.ppermute(x, ("seq", "dp"), hop(a)) for x in outward]
        here = flags[base + a]
        inward = [
            jnp.where(here > 0.5, g, 0.0 if e is None else e) for g, e in zip(got, inward)
        ]
        outward = [s + d * g for s, d, g in zip(sums, both, got)]
    for x, r, e, (my_decay, their_decay) in zip(mine, received, inward, cuts):
        if e is None:
            e = jnp.zeros_like(x)
        if sent:
            x, sent[-1] = lax.optimization_barrier((x, sent[-1]))
        through = jnp.where(first > 0.5, my_decay, their_decay) * e + jnp.where(first > 0.5, x, r)
        kept.append(jnp.where(first > 0.5, e, through))
        sent.append(jnp.where(first > 0.5, through, e))
    return kept, [lax.ppermute(x, "seq", swap) for x in sent]


def chunk_count(heads):
    return min(4, heads // 2)


def on_device(n_seq, n_dp, queries, keys, values, output_gradient, log_decay, gain):
    tok, width = queries.shape
    heads = log_decay.shape[0]
    dim = width // heads
    half = heads // 2
    chunks = chunk_count(heads)
    sizes = [half // chunks + (1 if i < half % chunks else 0) for i in range(chunks)]
    full_width = width * n_dp
    place = lax.axis_index("seq")
    pairs = n_seq // 2
    place = place.astype(jnp.int32).reshape(1)
    rows = -(-(1 + 2 * pairs) // 8) * 8
    gain_row = gain.reshape(1, width)
    pair_flops = 2 * tok * dim * dim
    state = [((n, dim, dim), f32) for n in sizes]
    row_bytes = tok * half * dim

    cum_t, cum_r, total, flags, *give = call(
        functools.partial(first_states, half, dim, pairs),
        [((tok, heads), f32), ((heads, tok), f32), ((heads, dim), f32), ((rows, dim), f32)] + state,
        2 * half * pair_flops, 8 * row_bytes,
    )(place, keys, values, log_decay)
    swap = [(i, i ^ 1) for i in range(n_seq)]
    other = lax.ppermute(total, "seq", swap)
    own_states = call(
        functools.partial(more_states, half, dim), state, 2 * half * pair_flops, 8 * row_bytes
    )(place, keys, values, cum_t)
    mixed, inner = call(
        functools.partial(within, heads, dim),
        [((heads, tok, tok), bf16), ((tok, width), f32)],
        2 * heads * pair_flops, 12 * row_bytes,
    )(place, queries, keys, values, cum_t, cum_r)

    upper = flags[0] > 0.5
    total_mine = jnp.where(upper, total[half:], total[:half])
    total_theirs = jnp.where(upper, other[half:], other[:half])
    in_own, in_give = carried(own_states, give, total_mine, total_theirs, flags, n_seq, n_dp, False)

    def outer(is_give, states, start, before, last):
        count = sum(x.shape[0] for x in states)
        return call(
            functools.partial(across, half, dim, is_give, start, len(before), last),
            [((tok, count * dim), f32), ((8, tok), f32) if last else ((2, tok, dim), f32)],
            2 * count * pair_flops, 14 * tok * count * dim,
        )(place, queries, inner, output_gradient, gain_row, cum_t, *before, *states)

    attn_own, part = outer(False, in_own, 0, [], False)
    early = sum(sizes[:-1])
    if early:
        attn_early, more = outer(True, in_give[:-1], 0, [part], False)
        attn_late, sums = outer(True, in_give[-1:], early, [more], True)
        attn_give = [attn_early, attn_late]
    else:
        attn_late, sums = outer(True, in_give, 0, [part], True)
        attn_give = [attn_late]

    if n_dp <= 4:
        all_sums = [sums] + [
            lax.ppermute(sums, "dp", [(i, i ^ m) for i in range(n_dp)]) for m in range(1, n_dp)
        ]
    else:
        all_sums = [lax.psum(sums, "dp")]

    def grads(is_give, attns):
        return call(
            functools.partial(gradient, half, dim, is_give, full_width, len(all_sums), len(attns)),
            [((tok, half * dim), bf16), ((half, dim), f32)] + state,
            2 * half * pair_flops, 14 * row_bytes,
        )(place, queries, output_gradient, gain_row, cum_t, *all_sums, *attns)

    d_give, gain_give, *back_give = grads(True, attn_give)
    d_own, gain_own, *back_own = grads(False, [attn_own])
    query_grad, key_part, value_part = call(
        functools.partial(local_grads, half, dim, chunks),
        [((tok, width), bf16), ((tok, width), f32), ((tok, width), f32)],
        6 * heads * pair_flops, 40 * row_bytes,
    )(place, queries, keys, values, cum_t, cum_r, mixed, d_own, d_give, *in_own, *in_give)

    late_own, late_give = carried(back_own, back_give, total_mine, total_theirs, flags, n_seq, n_dp, True)

    gain_grad = jnp.concatenate(
        [jnp.where(upper, gain_give, gain_own), jnp.where(upper, gain_own, gain_give)], axis=0
    )
    step = 1
    while step < n_seq:
        gain_grad = gain_grad + lax.ppermute(gain_grad, "seq", [(i, i ^ step) for i in range(n_seq)])
        step *= 2

    key_grad, value_grad = call(
        functools.partial(final_grads, half, dim, chunks),
        [((tok, width), bf16), ((tok, width), bf16)],
        4 * heads * pair_flops, 32 * row_bytes,
    )(place, keys, values, cum_t, key_part, value_part, *late_own, *late_give)
    return query_grad, key_grad, value_grad, gain_grad.reshape(width)


def solution(mesh):
    n_seq, n_dp = mesh.shape["seq"], mesh.shape["dp"]

    def body(*args):
        return on_device(n_seq, n_dp, *args)

    return jax.shard_map(
        body,
        mesh=mesh,
        in_specs=(P("seq", "dp"), P("seq", "dp"), P("seq", "dp"), P("seq", "dp"), P("dp", "seq"), P("dp")),
        out_specs=(P("seq", "dp"), P("seq", "dp"), P("seq", "dp"), P("dp")),
        check_vma=False,
    )
```

```python
import functools

import jax
import jax.numpy as jnp
from jax import lax
from jax.experimental import pallas as pl
from jax.experimental.pallas import tpu as pltpu
from jax.sharding import PartitionSpec as P


epsilon = 1e-05
highest = lax.Precision.HIGHEST
f32 = jnp.float32
bf16 = jnp.bfloat16
VMEM = pl.BlockSpec(memory_space=pltpu.VMEM)
SMEM = pl.BlockSpec(memory_space=pltpu.SMEM)
HBM = pl.BlockSpec(memory_space=pltpu.HBM)
GRANT = 24 * 2**20


def call(body, outs, flops, moved, in_hbm=(), outs_in_hbm=False, scratch=(), aliases=None):
    def run(place, *arrays):
        arrays = [pltpu.with_memory_space_constraint(x, pltpu.HBM) if i in in_hbm and not aliases else x for i, x in enumerate(arrays)]
        return pl.pallas_call(
            body,
            out_shape=[jax.ShapeDtypeStruct(*o) for o in outs],
            in_specs=[SMEM] + [HBM if i in in_hbm else VMEM for i in range(len(arrays))],
            out_specs=[HBM if outs_in_hbm else VMEM] * len(outs),
            scratch_shapes=list(scratch),
            input_output_aliases=aliases or {},
            compiler_params=pltpu.CompilerParams(vmem_limit_bytes=GRANT),
            cost_estimate=pl.CostEstimate(flops=flops, bytes_accessed=moved, transcendentals=0),
        )(place, *arrays)

    return run


def dot(a, b, ca, cb):
    return lax.dot_general(a, b, (((ca,), (cb,)), ((), ())), preferred_element_type=f32)


def split(x):
    hi = x.astype(bf16)
    return hi, (x - hi.astype(f32)).astype(bf16)


def column(table, side, half, j):
    return jnp.where(side == 0, table[:, j : j + 1], table[:, half + j : half + j + 1])


def side_of(place_ref, give):
    own = place_ref[0] & 1
    return 1 - own if give else own


def flags_of(place, pairs, shape):
    row = lax.broadcasted_iota(jnp.int32, shape, 0)
    odd, pair = place & 1, place >> 1
    forward = (row >= 3) & (row < 2 + pairs) & (row - 2 == pair)
    reverse = (row >= 2 + pairs) & (row < 1 + 2 * pairs) & (row - 1 - pairs == pairs - 1 - pair)
    even = jnp.full(shape, odd, jnp.int32) == 0
    on = ((row == 0) & ~even) | ((row == 1) & even) | ((row == 2) & ~even) | forward | reverse
    return on.astype(f32)


def lanes(side, half, j, dim):
    return pl.ds(pl.multiple_of((side * half + j) * dim, dim), dim)


def tables(ld):
    tok = ld.shape[1]
    row = lax.broadcasted_iota(jnp.int32, (tok, tok), 0)
    col = lax.broadcasted_iota(jnp.int32, (tok, tok), 1)
    lower = (row >= col).astype(f32)
    dims = (((1,), (1,)), ((), ()))
    cum_t = lax.dot_general(lower, ld, dims, precision=highest, preferred_element_type=f32)
    cum_r = lax.dot_general(ld, lower, dims, precision=highest, preferred_element_type=f32)
    return cum_t, cum_r


def state_into(outs, a_of, b_of, factor, side, half, start=0):
    j = start
    for out in outs:
        for i in range(out.shape[0]):
            hi, lo = split(a_of(j).astype(f32) * column(factor, side, half, j))
            b = b_of(j)
            out[i] = dot(hi, b, 0, 0) + dot(lo, b, 0, 0)
            j += 1


def first_states(half, dim, pairs, place_ref, k_ref, v_ref, ld_ref, cum_t_ref, cum_r_ref, total_ref, flags_ref, *refs):
    outs, (k_buf, v_buf, ld_buf, sems) = refs[:-4], refs[-4:]
    side = side_of(place_ref, True)
    copies = [pltpu.make_async_copy(ld_ref, ld_buf, sems.at[0])]
    at = 0
    for c, out in enumerate(outs):
        size = out.shape[0] * dim
        source = pl.ds(pl.multiple_of((side * half) * dim + at, dim), size)
        for n, (ref, buf) in enumerate(((k_ref, k_buf), (v_ref, v_buf))):
            copies.append(pltpu.make_async_copy(ref.at[:, source], buf.at[:, at : at + size], sems.at[1 + 2 * c + n]))
        at += size
    for copy in copies:
        copy.start()
    flags_ref[...] = flags_of(place_ref[0], pairs, flags_ref.shape)
    copies[0].wait()
    cum_t, cum_r = tables(ld_buf[...])
    cum_t_ref[...] = cum_t
    cum_r_ref[...] = cum_r
    tok = cum_t.shape[0]
    total_ref[...] = jnp.broadcast_to(jnp.exp(cum_r[:, tok - 1 :]), total_ref.shape)
    tail = jnp.exp(cum_t[tok - 1 :, :] - cum_t)
    start = 0
    for c, out in enumerate(outs):
        copies[1 + 2 * c].wait()
        copies[2 + 2 * c].wait()
        state_into(
            [out],
            lambda j: k_buf[:, j * dim : (j + 1) * dim],
            lambda j: v_buf[:, j * dim : (j + 1) * dim],
            tail, side, half, start,
        )
        start += out.shape[0]


def more_states(half, dim, place_ref, k_ref, v_ref, cum_t_ref, *outs):
    side = side_of(place_ref, False)
    cum_t = cum_t_ref[...]
    tail = jnp.exp(cum_t[cum_t.shape[0] - 1 :, :] - cum_t)
    state_into(
        outs,
        lambda j: k_ref[:, lanes(side, half, j, dim)],
        lambda j: v_ref[:, lanes(side, half, j, dim)],
        tail, side, half,
    )


def weights_of(cum_t, cum_r, h):
    tok = cum_t.shape[0]
    row = lax.broadcasted_iota(jnp.int32, (tok, tok), 0)
    col = lax.broadcasted_iota(jnp.int32, (tok, tok), 1)
    gap = cum_t[:, h : h + 1] - cum_r[h : h + 1, :]
    return jnp.where(row >= col, jnp.exp(jnp.minimum(gap, 0.0)), 0.0)


def within(heads, dim, place_ref, q_ref, k_ref, v_ref, cum_t_ref, cum_r_ref, mixed_ref, inner_ref):
    cum_t, cum_r = cum_t_ref[...], cum_r_ref[...]
    for h in range(heads):
        at = slice(h * dim, (h + 1) * dim)
        scores = dot(q_ref[:, at], k_ref[:, at], 1, 1)
        mixed = (scores * weights_of(cum_t, cum_r, h)).astype(bf16)
        mixed_ref[h] = mixed
        inner_ref[:, at] = dot(mixed, v_ref[:, at], 1, 0)


def across(half, dim, give, start, have, last, place_ref, *refs):
    side = side_of(place_ref, give)
    q_ref, inner_ref, g_ref, gain_ref, cum_t_ref = refs[:5]
    before = refs[5 : 5 + have]
    states = refs[5 + have : -2]
    attn_ref, sums_ref = refs[-2:]
    lead = jnp.exp(cum_t_ref[...])
    squares = cross = jnp.zeros((lead.shape[0], dim), f32)
    j = start
    for ref in states:
        for i in range(ref.shape[0]):
            at = lanes(side, half, j, dim)
            hi, lo = split(ref[i])
            q = q_ref[:, at]
            outer = (dot(q, hi, 1, 0) + dot(q, lo, 1, 0)) * column(lead, side, half, j)
            attn = inner_ref[:, at] + outer
            attn_ref[:, (j - start) * dim : (j - start + 1) * dim] = attn
            scaled = g_ref[:, at].astype(f32) * gain_ref[:, at]
            squares += attn * attn
            cross += scaled * attn
            j += 1
    for ref in before:
        squares += ref[0]
        cross += ref[1]
    if last:
        sums_ref[0:1, :] = jnp.sum(squares.T, axis=0, keepdims=True)
        sums_ref[1:2, :] = jnp.sum(cross.T, axis=0, keepdims=True)
        sums_ref[2:, :] = jnp.zeros((sums_ref.shape[0] - 2, sums_ref.shape[1]), f32)
    else:
        sums_ref[0] = squares
        sums_ref[1] = cross


def gradient(half, dim, give, full_width, n_sums, n_attn, place_ref, *refs):
    side = side_of(place_ref, give)
    q_ref, g_ref, gain_ref, cum_t_ref = refs[:4]
    sums = refs[4 : 4 + n_sums]
    attns = refs[4 + n_sums : 4 + n_sums + n_attn]
    d_ref, gain_part_ref = refs[4 + n_sums + n_attn :][:2]
    outs = refs[4 + n_sums + n_attn + 2 :]
    total = sums[0][...]
    for ref in sums[1:]:
        total = total + ref[...]
    inv_row = lax.rsqrt(total[0:1] / full_width + epsilon)
    mean_row = inv_row * (total[1:2] / full_width)
    tok = inv_row.shape[1]
    inv = jnp.broadcast_to(inv_row, (tok, tok)).T
    mean = jnp.broadcast_to(mean_row, (tok, tok)).T
    lead = jnp.exp(cum_t_ref[...])
    kept = {}
    j = 0
    for ref in attns:
        for i in range(ref.shape[1] // dim):
            at = lanes(side, half, j, dim)
            normed = ref[:, i * dim : (i + 1) * dim] * inv
            g = g_ref[:, at].astype(f32)
            d = (inv * (g * gain_ref[:, at] - normed * mean)).astype(bf16)
            d_ref[:, j * dim : (j + 1) * dim] = d
            gain_part_ref[j : j + 1, :] = jnp.sum(g * normed, axis=0, keepdims=True)
            kept[j] = d
            j += 1
    state_into(outs, lambda j: q_ref[:, lanes(side, half, j, dim)], lambda j: kept[j], lead, side, half)


def local_grads(half, dim, chunks, place_ref, *refs):
    side = side_of(place_ref, False)
    q_ref, k_ref, v_ref, cum_t_ref, cum_r_ref, mixed_ref, d_own_ref, d_give_ref = refs[:8]
    states = refs[8 : 8 + 2 * chunks]
    qg_ref, kg_ref, vg_ref = refs[8 + 2 * chunks :]
    cum_t = cum_t_ref[...]
    lead = jnp.exp(cum_t)
    tok = cum_t.shape[0]
    row = lax.broadcasted_iota(jnp.int32, (tok, tok), 0)
    col = lax.broadcasted_iota(jnp.int32, (tok, tok), 1)
    for s, (d_ref, group) in enumerate(((d_own_ref, states[:chunks]), (d_give_ref, states[chunks:]))):
        which = side if s == 0 else 1 - side
        j = 0
        for ref in group:
            for i in range(ref.shape[0]):
                at = lanes(which, half, j, dim)
                h = which * half + j
                d = d_ref[:, j * dim : (j + 1) * dim]
                cum_col = column(cum_t, which, half, j)
                gap = cum_col - cum_r_ref[pl.ds(h, 1), :]
                weights = jnp.where(row >= col, jnp.exp(jnp.minimum(gap, 0.0)), 0.0)
                graded = (dot(d, v_ref[:, at], 1, 1) * weights).astype(bf16)
                hi, lo = split(ref[i])
                outer = (dot(d, hi, 1, 1) + dot(d, lo, 1, 1)) * column(lead, which, half, j)
                qg_ref[:, at] = (dot(graded, k_ref[:, at], 1, 0) + outer).astype(bf16)
                kg_ref[:, at] = dot(graded, q_ref[:, at], 0, 0)
                vg_ref[:, at] = dot(mixed_ref[h], d, 0, 0)
                j += 1


def final_grads(half, dim, parts, skip, place_ref, *refs):
    k_ref, v_ref, cum_t_ref, kg_ref, vg_ref = refs[:5]
    states = refs[5 : 5 + len(parts)]
    key_ref, value_ref, key_buf, value_buf, sems = refs[5 + len(parts) + skip :]
    cum_t = cum_t_ref[...]
    tail = jnp.exp(cum_t[cum_t.shape[0] - 1 :, :] - cum_t)
    copies = []
    at = 0
    for n, (ref, (give, j)) in enumerate(zip(states, parts)):
        side = side_of(place_ref, give)
        size = ref.shape[0] * dim
        target = pl.ds(pl.multiple_of((side * half + j) * dim, dim), size)
        for i in range(ref.shape[0]):
            here = lanes(side, half, j + i, dim)
            to = slice(at + i * dim, at + (i + 1) * dim)
            tail_col = column(tail, side, half, j + i)
            hi, lo = split(ref[i])
            v, k = v_ref[:, here], k_ref[:, here]
            key_buf[:, to] = (kg_ref[:, here] + (dot(v, hi, 1, 1) + dot(v, lo, 1, 1)) * tail_col).astype(bf16)
            value_buf[:, to] = (vg_ref[:, here] + (dot(k, hi, 1, 0) + dot(k, lo, 1, 0)) * tail_col).astype(bf16)
        for m, (buf, out) in enumerate(((key_buf, key_ref), (value_buf, value_ref))):
            copies.append(pltpu.make_async_copy(buf.at[:, at : at + size], out.at[:, target], sems.at[2 * n + m]))
            copies[-1].start()
        at += size
    for copy in copies:
        copy.wait()


def carried(mine, theirs, total_mine, total_theirs, flags, n_seq, n_dp, reverse):
    pairs = n_seq // 2
    first = flags[2 if reverse else 1]
    base = 2 + pairs if reverse else 3
    swap = [(i, i ^ 1) for i in range(n_seq)]

    def hop(a):
        b = a + 1
        lo, hi = (pairs - 1 - a, pairs - 1 - b) if reverse else (a, b)
        perm = []
        for s in range(n_seq):
            for d in range(n_dp):
                if s // 2 == lo:
                    to = (s + 2 * (hi - lo)) * n_dp + d
                elif s // 2 == hi:
                    to = (s - 2 * (hi - lo)) * n_dp + d
                else:
                    to = s * n_dp + (d ^ 1)
                perm.append((s * n_dp + d, to))
        return perm

    received = [lax.ppermute(x, "seq", swap) for x in theirs]
    kept, sent = [], []
    at = 0
    cuts = []
    for x in mine:
        n = x.shape[0]
        cuts.append((total_mine[at : at + n, None, :], total_theirs[at : at + n, None, :]))
        at += n
    sums = [
        jnp.where(first > 0.5, their_decay, 1.0) * x + jnp.where(first > 0.5, 1.0, my_decay) * r
        for x, r, (my_decay, their_decay) in zip(mine, received, cuts)
    ]
    both = [a * b for a, b in cuts]
    inward = [None] * len(mine)
    outward = sums
    for a in range(pairs - 1):
        got = [lax.ppermute(x, ("seq", "dp"), hop(a)) for x in outward]
        here = flags[base + a]
        inward = [
            jnp.where(here > 0.5, g, 0.0 if e is None else e) for g, e in zip(got, inward)
        ]
        outward = [s + d * g for s, d, g in zip(sums, both, got)]
    for x, r, e, (my_decay, their_decay) in zip(mine, received, inward, cuts):
        if e is None:
            e = jnp.zeros_like(x)
        if sent:
            x, sent[-1] = lax.optimization_barrier((x, sent[-1]))
        through = jnp.where(first > 0.5, my_decay, their_decay) * e + jnp.where(first > 0.5, x, r)
        kept.append(jnp.where(first > 0.5, e, through))
        sent.append(jnp.where(first > 0.5, through, e))
    return kept, [lax.ppermute(x, "seq", swap) for x in sent]


def chunk_count(heads):
    return min(4, heads // 2)


def on_device(n_seq, n_dp, queries, keys, values, output_gradient, log_decay, gain):
    tok, width = queries.shape
    heads = log_decay.shape[0]
    dim = width // heads
    half = heads // 2
    chunks = chunk_count(heads)
    sizes = [half // chunks + (1 if i < half % chunks else 0) for i in range(chunks)]
    full_width = width * n_dp
    place = lax.axis_index("seq")
    pairs = n_seq // 2
    place = place.astype(jnp.int32).reshape(1)
    rows = -(-(1 + 2 * pairs) // 8) * 8
    gain_row = gain.reshape(1, width)
    pair_flops = 2 * tok * dim * dim
    state = [((n, dim, dim), f32) for n in sizes]
    row_bytes = tok * half * dim

    cum_t, cum_r, total, flags, *give = call(
        functools.partial(first_states, half, dim, pairs),
        [((tok, heads), f32), ((heads, tok), f32), ((heads, dim), f32), ((rows, dim), f32)] + state,
        2 * half * pair_flops, 8 * row_bytes,
        in_hbm=(0, 1, 2),
        scratch=[
            pltpu.VMEM((tok, half * dim), bf16),
            pltpu.VMEM((tok, half * dim), bf16),
            pltpu.VMEM((heads, tok), f32),
            pltpu.SemaphoreType.DMA((1 + 2 * chunks,)),
        ],
    )(place, keys, values, log_decay)
    swap = [(i, i ^ 1) for i in range(n_seq)]
    other = lax.ppermute(total, "seq", swap)
    own_states = call(
        functools.partial(more_states, half, dim), state, 2 * half * pair_flops, 8 * row_bytes
    )(place, keys, values, cum_t)
    mixed, inner = call(
        functools.partial(within, heads, dim),
        [((heads, tok, tok), bf16), ((tok, width), f32)],
        2 * heads * pair_flops, 12 * row_bytes,
    )(place, queries, keys, values, cum_t, cum_r)

    upper = flags[0] > 0.5
    total_mine = jnp.where(upper, total[half:], total[:half])
    total_theirs = jnp.where(upper, other[half:], other[:half])
    in_own, in_give = carried(own_states, give, total_mine, total_theirs, flags, n_seq, n_dp, False)

    def outer(is_give, states, start, before, last):
        count = sum(x.shape[0] for x in states)
        return call(
            functools.partial(across, half, dim, is_give, start, len(before), last),
            [((tok, count * dim), f32), ((8, tok), f32) if last else ((2, tok, dim), f32)],
            2 * count * pair_flops, 14 * tok * count * dim,
        )(place, queries, inner, output_gradient, gain_row, cum_t, *before, *states)

    attn_own, part = outer(False, in_own, 0, [], False)
    early = sum(sizes[:-1])
    if early:
        attn_early, more = outer(True, in_give[:-1], 0, [part], False)
        attn_late, sums = outer(True, in_give[-1:], early, [more], True)
        attn_give = [attn_early, attn_late]
    else:
        attn_late, sums = outer(True, in_give, 0, [part], True)
        attn_give = [attn_late]

    if n_dp <= 4:
        all_sums = [sums] + [
            lax.ppermute(sums, "dp", [(i, i ^ m) for i in range(n_dp)]) for m in range(1, n_dp)
        ]
    else:
        all_sums = [lax.psum(sums, "dp")]

    def grads(is_give, attns):
        return call(
            functools.partial(gradient, half, dim, is_give, full_width, len(all_sums), len(attns)),
            [((tok, half * dim), bf16), ((half, dim), f32)] + state,
            2 * half * pair_flops, 14 * row_bytes,
        )(place, queries, output_gradient, gain_row, cum_t, *all_sums, *attns)

    d_give, gain_give, *back_give = grads(True, attn_give)
    d_own, gain_own, *back_own = grads(False, [attn_own])
    query_grad, key_part, value_part = call(
        functools.partial(local_grads, half, dim, chunks),
        [((tok, width), bf16), ((tok, width), f32), ((tok, width), f32)],
        6 * heads * pair_flops, 40 * row_bytes,
    )(place, queries, keys, values, cum_t, cum_r, mixed, d_own, d_give, *in_own, *in_give)

    late_own, late_give = carried(back_own, back_give, total_mine, total_theirs, flags, n_seq, n_dp, True)

    gain_grad = jnp.concatenate(
        [jnp.where(upper, gain_give, gain_own), jnp.where(upper, gain_own, gain_give)], axis=0
    )
    step = 1
    while step < n_seq:
        gain_grad = gain_grad + lax.ppermute(gain_grad, "seq", [(i, i ^ step) for i in range(n_seq)])
        step *= 2

    places = [sum(sizes[:c]) for c in range(chunks)]

    def finish(parts, states, before):
        count = sum(x.shape[0] for x in states)
        return call(
            functools.partial(final_grads, half, dim, parts, len(before)),
            [((tok, width), bf16), ((tok, width), bf16)],
            4 * count * pair_flops, 20 * tok * count * dim,
            in_hbm=range(5 + len(parts), 7 + len(parts)),
            outs_in_hbm=True,
            scratch=[
                pltpu.VMEM((tok, count * dim), bf16),
                pltpu.VMEM((tok, count * dim), bf16),
                pltpu.SemaphoreType.DMA((2 * len(parts),)),
            ],
            aliases={6 + len(parts): 0, 7 + len(parts): 1} if before else None,
        )(place, keys, values, cum_t, key_part, value_part, *states, *before)

    own_parts = [(False, p) for p in places]
    give_parts = [(True, p) for p in places]
    begun = finish(own_parts + give_parts[:-1], late_own + late_give[:-1], [])
    key_grad, value_grad = finish(give_parts[-1:], late_give[-1:], list(begun))
    return query_grad, key_grad, value_grad, gain_grad.reshape(width)


def solution(mesh):
    n_seq, n_dp = mesh.shape["seq"], mesh.shape["dp"]

    def body(*args):
        return on_device(n_seq, n_dp, *args)

    return jax.shard_map(
        body,
        mesh=mesh,
        in_specs=(P("seq", "dp"), P("seq", "dp"), P("seq", "dp"), P("seq", "dp"), P("dp", "seq"), P("dp")),
        out_specs=(P("seq", "dp"), P("seq", "dp"), P("seq", "dp"), P("dp")),
        check_vma=False,
    )
```

```python
import functools

import jax
import jax.numpy as jnp
from jax import lax
from jax.experimental import pallas as pl
from jax.experimental.pallas import tpu as pltpu
from jax.sharding import PartitionSpec as P


epsilon = 1e-05
highest = lax.Precision.HIGHEST
f32 = jnp.float32
bf16 = jnp.bfloat16
VMEM = pl.BlockSpec(memory_space=pltpu.VMEM)
SMEM = pl.BlockSpec(memory_space=pltpu.SMEM)
HBM = pl.BlockSpec(memory_space=pltpu.HBM)
GRANT = 24 * 2**20


def call(body, outs, flops, moved, in_hbm=(), outs_in_hbm=(), scratch=(), aliases=None):
    def run(place, *arrays):
        arrays = [pltpu.with_memory_space_constraint(x, pltpu.HBM) if i in in_hbm and not aliases else x for i, x in enumerate(arrays)]
        return pl.pallas_call(
            body,
            out_shape=[jax.ShapeDtypeStruct(*o) for o in outs],
            in_specs=[SMEM] + [HBM if i in in_hbm else VMEM for i in range(len(arrays))],
            out_specs=[HBM if i in outs_in_hbm else VMEM for i in range(len(outs))],
            scratch_shapes=list(scratch),
            input_output_aliases=aliases or {},
            compiler_params=pltpu.CompilerParams(vmem_limit_bytes=GRANT),
            cost_estimate=pl.CostEstimate(flops=flops, bytes_accessed=moved, transcendentals=0),
        )(place, *arrays)

    return run


def dot(a, b, ca, cb):
    return lax.dot_general(a, b, (((ca,), (cb,)), ((), ())), preferred_element_type=f32)


def split(x):
    hi = x.astype(bf16)
    return hi, (x - hi.astype(f32)).astype(bf16)


def column(table, side, half, j):
    return jnp.where(side == 0, table[:, j : j + 1], table[:, half + j : half + j + 1])


def side_of(place_ref, give):
    own = place_ref[0] & 1
    return 1 - own if give else own


def flags_of(place, pairs, shape):
    row = lax.broadcasted_iota(jnp.int32, shape, 0)
    odd, pair = place & 1, place >> 1
    forward = (row >= 3) & (row < 2 + pairs) & (row - 2 == pair)
    reverse = (row >= 2 + pairs) & (row < 1 + 2 * pairs) & (row - 1 - pairs == pairs - 1 - pair)
    even = jnp.full(shape, odd, jnp.int32) == 0
    on = ((row == 0) & ~even) | ((row == 1) & even) | ((row == 2) & ~even) | forward | reverse
    return on.astype(f32)


def lanes(side, half, j, dim):
    return pl.ds(pl.multiple_of((side * half + j) * dim, dim), dim)


def tables(ld):
    tok = ld.shape[1]
    row = lax.broadcasted_iota(jnp.int32, (tok, tok), 0)
    col = lax.broadcasted_iota(jnp.int32, (tok, tok), 1)
    lower = (row >= col).astype(f32)
    dims = (((1,), (1,)), ((), ()))
    cum_t = lax.dot_general(lower, ld, dims, precision=highest, preferred_element_type=f32)
    cum_r = lax.dot_general(ld, lower, dims, precision=highest, preferred_element_type=f32)
    return cum_t, cum_r


def state_into(outs, a_of, b_of, factor, side, half, start=0):
    j = start
    for out in outs:
        for i in range(out.shape[0]):
            hi, lo = split(a_of(j).astype(f32) * column(factor, side, half, j))
            b = b_of(j)
            out[i] = dot(hi, b, 0, 0) + dot(lo, b, 0, 0)
            j += 1


def first_states(half, dim, pairs, place_ref, k_ref, v_ref, ld_ref, cum_t_ref, cum_r_ref, total_ref, flags_ref, *refs):
    outs, (k_buf, v_buf, ld_buf, sems) = refs[:-4], refs[-4:]
    side = side_of(place_ref, True)
    copies = [pltpu.make_async_copy(ld_ref, ld_buf, sems.at[0])]
    at = 0
    for c, out in enumerate(outs):
        size = out.shape[0] * dim
        source = pl.ds(pl.multiple_of((side * half) * dim + at, dim), size)
        for n, (ref, buf) in enumerate(((k_ref, k_buf), (v_ref, v_buf))):
            copies.append(pltpu.make_async_copy(ref.at[:, source], buf.at[:, at : at + size], sems.at[1 + 2 * c + n]))
        at += size
    for copy in copies:
        copy.start()
    flags_ref[...] = flags_of(place_ref[0], pairs, flags_ref.shape)
    copies[0].wait()
    cum_t, cum_r = tables(ld_buf[...])
    cum_t_ref[...] = cum_t
    cum_r_ref[...] = cum_r
    tok = cum_t.shape[0]
    total_ref[...] = jnp.broadcast_to(jnp.exp(cum_r[:, tok - 1 :]), total_ref.shape)
    tail = jnp.exp(cum_t[tok - 1 :, :] - cum_t)
    start = 0
    for c, out in enumerate(outs):
        copies[1 + 2 * c].wait()
        copies[2 + 2 * c].wait()
        state_into(
            [out],
            lambda j: k_buf[:, j * dim : (j + 1) * dim],
            lambda j: v_buf[:, j * dim : (j + 1) * dim],
            tail, side, half, start,
        )
        start += out.shape[0]


def more_states(half, dim, place_ref, k_ref, v_ref, cum_t_ref, *outs):
    side = side_of(place_ref, False)
    cum_t = cum_t_ref[...]
    tail = jnp.exp(cum_t[cum_t.shape[0] - 1 :, :] - cum_t)
    state_into(
        outs,
        lambda j: k_ref[:, lanes(side, half, j, dim)],
        lambda j: v_ref[:, lanes(side, half, j, dim)],
        tail, side, half,
    )


def weights_of(cum_t, cum_r_ref, side, half, j):
    tok = cum_t.shape[0]
    row = lax.broadcasted_iota(jnp.int32, (tok, tok), 0)
    col = lax.broadcasted_iota(jnp.int32, (tok, tok), 1)
    gap = column(cum_t, side, half, j) - cum_r_ref[pl.ds(side * half + j, 1), :]
    return jnp.where(row >= col, jnp.exp(jnp.minimum(gap, 0.0)), 0.0)


def within(half, dim, give, start, place_ref, q_ref, k_ref, v_ref, cum_t_ref, cum_r_ref, mixed_ref, inner_ref):
    side = side_of(place_ref, give)
    cum_t = cum_t_ref[...]
    for i in range(mixed_ref.shape[0]):
        at = lanes(side, half, start + i, dim)
        scores = dot(q_ref[:, at], k_ref[:, at], 1, 1)
        mixed = (scores * weights_of(cum_t, cum_r_ref, side, half, start + i)).astype(bf16)
        mixed_ref[i] = mixed
        inner_ref[:, i * dim : (i + 1) * dim] = dot(mixed, v_ref[:, at], 1, 0)


def across(half, dim, give, start, inners, have, last, place_ref, *refs):
    side = side_of(place_ref, give)
    q_ref, g_ref, gain_ref, cum_t_ref = refs[:4]
    inner = [ref[:, i * dim : (i + 1) * dim] for ref in refs[4 : 4 + inners] for i in range(ref.shape[1] // dim)]
    before = refs[4 + inners : 4 + inners + have]
    states = refs[4 + inners + have : -2]
    attn_ref, sums_ref = refs[-2:]
    lead = jnp.exp(cum_t_ref[...])
    squares = cross = jnp.zeros((lead.shape[0], dim), f32)
    j = start
    for ref in states:
        for i in range(ref.shape[0]):
            at = lanes(side, half, j, dim)
            hi, lo = split(ref[i])
            q = q_ref[:, at]
            outer = (dot(q, hi, 1, 0) + dot(q, lo, 1, 0)) * column(lead, side, half, j)
            attn = inner[j] + outer
            attn_ref[:, (j - start) * dim : (j - start + 1) * dim] = attn
            scaled = g_ref[:, at].astype(f32) * gain_ref[:, at]
            squares += attn * attn
            cross += scaled * attn
            j += 1
    for ref in before:
        squares += ref[0]
        cross += ref[1]
    if last:
        sums_ref[0:1, :] = jnp.sum(squares.T, axis=0, keepdims=True)
        sums_ref[1:2, :] = jnp.sum(cross.T, axis=0, keepdims=True)
        sums_ref[2:, :] = jnp.zeros((sums_ref.shape[0] - 2, sums_ref.shape[1]), f32)
    else:
        sums_ref[0] = squares
        sums_ref[1] = cross


def gradient(half, dim, give, full_width, n_sums, n_attn, place_ref, *refs):
    side = side_of(place_ref, give)
    q_ref, g_ref, gain_ref, cum_t_ref = refs[:4]
    sums = refs[4 : 4 + n_sums]
    attns = refs[4 + n_sums : 4 + n_sums + n_attn]
    d_ref, gain_part_ref = refs[4 + n_sums + n_attn :][:2]
    outs = refs[4 + n_sums + n_attn + 2 :]
    total = sums[0][...]
    for ref in sums[1:]:
        total = total + ref[...]
    inv_row = lax.rsqrt(total[0:1] / full_width + epsilon)
    mean_row = inv_row * (total[1:2] / full_width)
    tok = inv_row.shape[1]
    inv = jnp.broadcast_to(inv_row, (tok, tok)).T
    mean = jnp.broadcast_to(mean_row, (tok, tok)).T
    lead = jnp.exp(cum_t_ref[...])
    kept = {}
    j = 0
    for ref in attns:
        for i in range(ref.shape[1] // dim):
            at = lanes(side, half, j, dim)
            normed = ref[:, i * dim : (i + 1) * dim] * inv
            g = g_ref[:, at].astype(f32)
            d = (inv * (g * gain_ref[:, at] - normed * mean)).astype(bf16)
            d_ref[:, j * dim : (j + 1) * dim] = d
            gain_part_ref[j : j + 1, :] = jnp.sum(g * normed, axis=0, keepdims=True)
            kept[j] = d
            j += 1
    state_into(outs, lambda j: q_ref[:, lanes(side, half, j, dim)], lambda j: kept[j], lead, side, half)


def local_grads(half, dim, give, start, place_ref, *refs):
    side = side_of(place_ref, give)
    q_ref, k_ref, v_ref, cum_t_ref, cum_r_ref, mixed_ref, d_ref = refs[:7]
    query_ref, kg_ref, vg_ref = refs[-3:]
    cum_t = cum_t_ref[...]
    lead = jnp.exp(cum_t)
    count = 0
    for ref in refs[7:-3]:
        for n in range(ref.shape[0]):
            j = start + count
            at = lanes(side, half, j, dim)
            to = slice(count * dim, (count + 1) * dim)
            d = d_ref[:, j * dim : (j + 1) * dim]
            graded = (dot(d, v_ref[:, at], 1, 1) * weights_of(cum_t, cum_r_ref, side, half, j)).astype(bf16)
            hi, lo = split(ref[n])
            outer = (dot(d, hi, 1, 1) + dot(d, lo, 1, 1)) * column(lead, side, half, j)
            query_ref[:, to] = (dot(graded, k_ref[:, at], 1, 0) + outer).astype(bf16)
            kg_ref[:, to] = dot(graded, q_ref[:, at], 0, 0)
            vg_ref[:, to] = dot(mixed_ref[count], d, 0, 0)
            count += 1


def final_grads(half, dim, parts, pieces, queries, skip, place_ref, *refs):
    k_ref, v_ref, cum_t_ref = refs[:3]
    refs = refs[3:]
    local = {}
    for (give, first), kg_ref, vg_ref in zip(pieces, refs[::2], refs[1::2]):
        for i in range(kg_ref.shape[1] // dim):
            local[give, first + i] = (kg_ref, vg_ref, slice(i * dim, (i + 1) * dim))
    refs = refs[2 * len(pieces) :]
    states, query_pieces = refs[: len(parts)], refs[len(parts) : len(parts) + len(queries)]
    outs = refs[len(parts) + len(queries) + skip :]
    key_ref, value_ref = outs[:2]
    key_buf, value_buf, sems = outs[-3:]
    cum_t = cum_t_ref[...]
    tail = jnp.exp(cum_t[cum_t.shape[0] - 1 :, :] - cum_t)
    copies = []

    def put(source, out, give, j):
        side = side_of(place_ref, give)
        target = pl.ds(pl.multiple_of((side * half + j) * dim, dim), source.shape[1])
        copies.append(pltpu.make_async_copy(source, out.at[:, target], sems.at[len(copies)]))
        copies[-1].start()

    for ref, (give, j) in zip(query_pieces, queries):
        put(ref, outs[2], give, j)
    at = 0
    for ref, (give, j) in zip(states, parts):
        side = side_of(place_ref, give)
        size = ref.shape[0] * dim
        for i in range(ref.shape[0]):
            here = lanes(side, half, j + i, dim)
            to = slice(at + i * dim, at + (i + 1) * dim)
            tail_col = column(tail, side, half, j + i)
            hi, lo = split(ref[i])
            v, k = v_ref[:, here], k_ref[:, here]
            kg_ref, vg_ref, part = local[give, j + i]
            key_buf[:, to] = (kg_ref[:, part] + (dot(v, hi, 1, 1) + dot(v, lo, 1, 1)) * tail_col).astype(bf16)
            value_buf[:, to] = (vg_ref[:, part] + (dot(k, hi, 1, 0) + dot(k, lo, 1, 0)) * tail_col).astype(bf16)
        put(key_buf.at[:, at : at + size], key_ref, give, j)
        put(value_buf.at[:, at : at + size], value_ref, give, j)
        at += size
    for copy in copies:
        copy.wait()


def carried(mine, theirs, total_mine, total_theirs, flags, n_seq, n_dp, reverse):
    pairs = n_seq // 2
    first = flags[2 if reverse else 1]
    base = 2 + pairs if reverse else 3
    swap = [(i, i ^ 1) for i in range(n_seq)]

    def hop(a):
        b = a + 1
        lo, hi = (pairs - 1 - a, pairs - 1 - b) if reverse else (a, b)
        perm = []
        for s in range(n_seq):
            for d in range(n_dp):
                if s // 2 == lo:
                    to = (s + 2 * (hi - lo)) * n_dp + d
                elif s // 2 == hi:
                    to = (s - 2 * (hi - lo)) * n_dp + d
                else:
                    to = s * n_dp + (d ^ 1)
                perm.append((s * n_dp + d, to))
        return perm

    received = [lax.ppermute(x, "seq", swap) for x in theirs]
    kept, sent = [], []
    at = 0
    cuts = []
    for x in mine:
        n = x.shape[0]
        cuts.append((total_mine[at : at + n, None, :], total_theirs[at : at + n, None, :]))
        at += n
    sums = [
        jnp.where(first > 0.5, their_decay, 1.0) * x + jnp.where(first > 0.5, 1.0, my_decay) * r
        for x, r, (my_decay, their_decay) in zip(mine, received, cuts)
    ]
    both = [a * b for a, b in cuts]
    inward = [None] * len(mine)
    outward = sums
    for a in range(pairs - 1):
        got = [lax.ppermute(x, ("seq", "dp"), hop(a)) for x in outward]
        here = flags[base + a]
        inward = [
            jnp.where(here > 0.5, g, 0.0 if e is None else e) for g, e in zip(got, inward)
        ]
        outward = [s + d * g for s, d, g in zip(sums, both, got)]
    for x, r, e, (my_decay, their_decay) in zip(mine, received, inward, cuts):
        if e is None:
            e = jnp.zeros_like(x)
        if sent:
            x, sent[-1] = lax.optimization_barrier((x, sent[-1]))
        through = jnp.where(first > 0.5, my_decay, their_decay) * e + jnp.where(first > 0.5, x, r)
        kept.append(jnp.where(first > 0.5, e, through))
        sent.append(jnp.where(first > 0.5, through, e))
    return kept, [lax.ppermute(x, "seq", swap) for x in sent]


def chunk_count(heads):
    return min(4, heads // 2)


def on_device(n_seq, n_dp, queries, keys, values, output_gradient, log_decay, gain):
    tok, width = queries.shape
    heads = log_decay.shape[0]
    dim = width // heads
    half = heads // 2
    chunks = chunk_count(heads)
    sizes = [half // chunks + (1 if i < half % chunks else 0) for i in range(chunks)]
    full_width = width * n_dp
    place = lax.axis_index("seq")
    pairs = n_seq // 2
    place = place.astype(jnp.int32).reshape(1)
    rows = -(-(1 + 2 * pairs) // 8) * 8
    gain_row = gain.reshape(1, width)
    pair_flops = 2 * tok * dim * dim
    state = [((n, dim, dim), f32) for n in sizes]
    row_bytes = tok * half * dim

    cum_t, cum_r, total, flags, *give = call(
        functools.partial(first_states, half, dim, pairs),
        [((tok, heads), f32), ((heads, tok), f32), ((heads, dim), f32), ((rows, dim), f32)] + state,
        2 * half * pair_flops, 8 * row_bytes,
        in_hbm=(0, 1, 2),
        scratch=[
            pltpu.VMEM((tok, half * dim), bf16),
            pltpu.VMEM((tok, half * dim), bf16),
            pltpu.VMEM((heads, tok), f32),
            pltpu.SemaphoreType.DMA((1 + 2 * chunks,)),
        ],
    )(place, keys, values, log_decay)
    swap = [(i, i ^ 1) for i in range(n_seq)]
    other = lax.ppermute(total, "seq", swap)
    own_states = call(
        functools.partial(more_states, half, dim), state, 2 * half * pair_flops, 8 * row_bytes
    )(place, keys, values, cum_t)
    places = [sum(sizes[:c]) for c in range(chunks)]
    middle = (chunks + 1) // 2
    pieces = [
        (give_piece, run)
        for give_piece in (False, True)
        for run in (list(range(middle)), list(range(middle, chunks)))
        if run
    ]
    mixed, inner = [], {False: [], True: []}
    for is_give, run in pieces:
        count = sum(sizes[c] for c in run)
        mix, inn = call(
            functools.partial(within, half, dim, is_give, places[run[0]]),
            [((count, tok, tok), bf16), ((tok, count * dim), f32)],
            2 * count * pair_flops, 12 * tok * count * dim,
        )(place, queries, keys, values, cum_t, cum_r)
        mixed.append(mix)
        inner[is_give].append(inn)

    upper = flags[0] > 0.5
    total_mine = jnp.where(upper, total[half:], total[:half])
    total_theirs = jnp.where(upper, other[half:], other[:half])
    in_own, in_give = carried(own_states, give, total_mine, total_theirs, flags, n_seq, n_dp, False)

    def outer(is_give, states, start, before, last):
        count = sum(x.shape[0] for x in states)
        return call(
            functools.partial(across, half, dim, is_give, start, len(inner[is_give]), len(before), last),
            [((tok, count * dim), f32), ((8, tok), f32) if last else ((2, tok, dim), f32)],
            2 * count * pair_flops, 14 * tok * count * dim,
        )(place, queries, output_gradient, gain_row, cum_t, *inner[is_give], *before, *states)

    attn_own, part = outer(False, in_own, 0, [], False)
    early = sum(sizes[:-1])
    if early:
        attn_early, more = outer(True, in_give[:-1], 0, [part], False)
        attn_late, sums = outer(True, in_give[-1:], early, [more], True)
        attn_give = [attn_early, attn_late]
    else:
        attn_late, sums = outer(True, in_give, 0, [part], True)
        attn_give = [attn_late]

    if n_dp <= 4:
        all_sums = [sums] + [
            lax.ppermute(sums, "dp", [(i, i ^ m) for i in range(n_dp)]) for m in range(1, n_dp)
        ]
    else:
        all_sums = [lax.psum(sums, "dp")]

    def grads(is_give, attns):
        return call(
            functools.partial(gradient, half, dim, is_give, full_width, len(all_sums), len(attns)),
            [((tok, half * dim), bf16), ((half, dim), f32)] + state,
            2 * half * pair_flops, 14 * row_bytes,
        )(place, queries, output_gradient, gain_row, cum_t, *all_sums, *attns)

    d_give, gain_give, *back_give = grads(True, attn_give)
    d_own, gain_own, *back_own = grads(False, [attn_own])
    query_pieces, local = [], []
    for n, (is_give, run) in enumerate(pieces):
        count = sum(sizes[c] for c in run)
        states = [(in_give if is_give else in_own)[c] for c in run]
        query, key_part, value_part = call(
            functools.partial(local_grads, half, dim, is_give, places[run[0]]),
            [((tok, count * dim), bf16), ((tok, count * dim), f32), ((tok, count * dim), f32)],
            6 * count * pair_flops, 40 * tok * count * dim,
        )(place, queries, keys, values, cum_t, cum_r, mixed[n], d_give if is_give else d_own, *states)
        query_pieces.append(((is_give, places[run[0]]), query))
        local.append(((is_give, places[run[0]]), key_part, value_part))

    late_own, late_give = carried(back_own, back_give, total_mine, total_theirs, flags, n_seq, n_dp, True)

    gain_grad = jnp.concatenate(
        [jnp.where(upper, gain_give, gain_own), jnp.where(upper, gain_own, gain_give)], axis=0
    )
    step = 1
    while step < n_seq:
        gain_grad = gain_grad + lax.ppermute(gain_grad, "seq", [(i, i ^ step) for i in range(n_seq)])
        step *= 2

    def finish(parts, states, query_parts, before):
        count = sum(x.shape[0] for x in states)
        used = [
            (mark, key_part, value_part)
            for mark, key_part, value_part in local
            if any(mark[0] == g and mark[1] <= p < mark[1] + key_part.shape[1] // dim for g, p in parts)
        ]
        base = 3 + 2 * len(used) + len(parts) + len(query_parts)
        outs = 3 if query_parts else 2
        return call(
            functools.partial(
                final_grads, half, dim, parts, [u[0] for u in used], [q for q, _ in query_parts], len(before)
            ),
            [((tok, width), bf16)] * outs,
            4 * count * pair_flops, 20 * tok * count * dim,
            in_hbm=(base, base + 1),
            outs_in_hbm=range(outs),
            scratch=[
                pltpu.VMEM((tok, count * dim), bf16),
                pltpu.VMEM((tok, count * dim), bf16),
                pltpu.SemaphoreType.DMA((2 * len(parts) + len(query_parts),)),
            ],
            aliases={base + 1: 0, base + 2: 1} if before else None,
        )(
            place, keys, values, cum_t, *[x for _, a, b in used for x in (a, b)], *states,
            *[q for _, q in query_parts], *before,
        )

    own_parts = [(False, p) for p in places]
    give_parts = [(True, p) for p in places]
    begun = finish(own_parts, late_own, [], [])
    if chunks > 1:
        *begun, query_grad = finish(give_parts[:-1], late_give[:-1], query_pieces, begun)
        key_grad, value_grad = finish(give_parts[-1:], late_give[-1:], [], begun)
    else:
        key_grad, value_grad, query_grad = finish(give_parts, late_give, query_pieces, begun)
    return query_grad, key_grad, value_grad, gain_grad.reshape(width)


def solution(mesh):
    n_seq, n_dp = mesh.shape["seq"], mesh.shape["dp"]

    def body(*args):
        return on_device(n_seq, n_dp, *args)

    return jax.shard_map(
        body,
        mesh=mesh,
        in_specs=(P("seq", "dp"), P("seq", "dp"), P("seq", "dp"), P("seq", "dp"), P("dp", "seq"), P("dp")),
        out_specs=(P("seq", "dp"), P("seq", "dp"), P("seq", "dp"), P("dp")),
        check_vma=False,
    )
```

```python
import functools

import jax
import jax.numpy as jnp
from jax import lax
from jax.experimental import pallas as pl
from jax.experimental.pallas import tpu as pltpu
from jax.sharding import PartitionSpec as P


epsilon = 1e-05
highest = lax.Precision.HIGHEST
f32 = jnp.float32
bf16 = jnp.bfloat16
VMEM = pl.BlockSpec(memory_space=pltpu.VMEM)
SMEM = pl.BlockSpec(memory_space=pltpu.SMEM)
HBM = pl.BlockSpec(memory_space=pltpu.HBM)
GRANT = 24 * 2**20


def call(body, outs, flops, moved, in_hbm=(), outs_in_hbm=(), scratch=(), aliases=None):
    def run(place, *arrays):
        arrays = [pltpu.with_memory_space_constraint(x, pltpu.HBM) if i in in_hbm and not aliases else x for i, x in enumerate(arrays)]
        return pl.pallas_call(
            body,
            out_shape=[jax.ShapeDtypeStruct(*o) for o in outs],
            in_specs=[SMEM] + [HBM if i in in_hbm else VMEM for i in range(len(arrays))],
            out_specs=[HBM if i in outs_in_hbm else VMEM for i in range(len(outs))],
            scratch_shapes=list(scratch),
            input_output_aliases=aliases or {},
            compiler_params=pltpu.CompilerParams(vmem_limit_bytes=GRANT),
            cost_estimate=pl.CostEstimate(flops=flops, bytes_accessed=moved, transcendentals=0),
        )(place, *arrays)

    return run


def dot(a, b, ca, cb):
    return lax.dot_general(a, b, (((ca,), (cb,)), ((), ())), preferred_element_type=f32)


def split(x):
    hi = x.astype(bf16)
    return hi, (x - hi.astype(f32)).astype(bf16)


def column(table, side, half, j):
    return jnp.where(side == 0, table[:, j : j + 1], table[:, half + j : half + j + 1])


def side_of(place_ref, give):
    own = place_ref[0] & 1
    return 1 - own if give else own


def flags_of(place, pairs, shape):
    row = lax.broadcasted_iota(jnp.int32, shape, 0)
    odd, pair = place & 1, place >> 1
    forward = (row >= 3) & (row < 2 + pairs) & (row - 2 == pair)
    reverse = (row >= 2 + pairs) & (row < 1 + 2 * pairs) & (row - 1 - pairs == pairs - 1 - pair)
    even = jnp.full(shape, odd, jnp.int32) == 0
    on = ((row == 0) & ~even) | ((row == 1) & even) | ((row == 2) & ~even) | forward | reverse
    return on.astype(f32)


def lanes(side, half, j, dim):
    return pl.ds(pl.multiple_of((side * half + j) * dim, dim), dim)


def tables(ld):
    tok = ld.shape[1]
    row = lax.broadcasted_iota(jnp.int32, (tok, tok), 0)
    col = lax.broadcasted_iota(jnp.int32, (tok, tok), 1)
    lower = (row >= col).astype(f32)
    dims = (((1,), (1,)), ((), ()))
    cum_t = lax.dot_general(lower, ld, dims, precision=highest, preferred_element_type=f32)
    cum_r = lax.dot_general(ld, lower, dims, precision=highest, preferred_element_type=f32)
    return cum_t, cum_r


def state_into(outs, a_of, b_of, factor, side, half, start=0):
    j = start
    for out in outs:
        for i in range(out.shape[0]):
            hi, lo = split(a_of(j).astype(f32) * column(factor, side, half, j))
            b = b_of(j)
            out[i] = dot(hi, b, 0, 0) + dot(lo, b, 0, 0)
            j += 1


def first_states(half, dim, pairs, place_ref, k_ref, v_ref, ld_ref, cum_t_ref, cum_r_ref, total_ref, flags_ref, *refs):
    outs, (k_buf, v_buf, ld_buf, sems) = refs[:-4], refs[-4:]
    side = side_of(place_ref, True)
    copies = [pltpu.make_async_copy(ld_ref, ld_buf, sems.at[0])]
    at = 0
    for c, out in enumerate(outs):
        size = out.shape[0] * dim
        source = pl.ds(pl.multiple_of((side * half) * dim + at, dim), size)
        for n, (ref, buf) in enumerate(((k_ref, k_buf), (v_ref, v_buf))):
            copies.append(pltpu.make_async_copy(ref.at[:, source], buf.at[:, at : at + size], sems.at[1 + 2 * c + n]))
        at += size
    for copy in copies:
        copy.start()
    flags_ref[...] = flags_of(place_ref[0], pairs, flags_ref.shape)
    copies[0].wait()
    cum_t, cum_r = tables(ld_buf[...])
    cum_t_ref[...] = cum_t
    cum_r_ref[...] = cum_r
    tok = cum_t.shape[0]
    total_ref[...] = jnp.broadcast_to(jnp.exp(cum_r[:, tok - 1 :]), total_ref.shape)
    tail = jnp.exp(cum_t[tok - 1 :, :] - cum_t)
    start = 0
    for c, out in enumerate(outs):
        copies[1 + 2 * c].wait()
        copies[2 + 2 * c].wait()
        state_into(
            [out],
            lambda j: k_buf[:, j * dim : (j + 1) * dim],
            lambda j: v_buf[:, j * dim : (j + 1) * dim],
            tail, side, half, start,
        )
        start += out.shape[0]


def more_states(half, dim, place_ref, k_ref, v_ref, cum_t_ref, *outs):
    side = side_of(place_ref, False)
    cum_t = cum_t_ref[...]
    tail = jnp.exp(cum_t[cum_t.shape[0] - 1 :, :] - cum_t)
    state_into(
        outs,
        lambda j: k_ref[:, lanes(side, half, j, dim)],
        lambda j: v_ref[:, lanes(side, half, j, dim)],
        tail, side, half,
    )


def weights_of(cum_t, cum_r_ref, side, half, j):
    tok = cum_t.shape[0]
    row = lax.broadcasted_iota(jnp.int32, (tok, tok), 0)
    col = lax.broadcasted_iota(jnp.int32, (tok, tok), 1)
    gap = column(cum_t, side, half, j) - cum_r_ref[pl.ds(side * half + j, 1), :]
    return jnp.where(row >= col, jnp.exp(jnp.minimum(gap, 0.0)), 0.0)


def within(half, dim, give, start, place_ref, q_ref, k_ref, v_ref, cum_t_ref, cum_r_ref, mixed_ref, inner_ref):
    side = side_of(place_ref, give)
    cum_t = cum_t_ref[...]
    for i in range(mixed_ref.shape[0]):
        at = lanes(side, half, start + i, dim)
        scores = dot(q_ref[:, at], k_ref[:, at], 1, 1)
        mixed = (scores * weights_of(cum_t, cum_r_ref, side, half, start + i)).astype(bf16)
        mixed_ref[i] = mixed
        inner_ref[:, i * dim : (i + 1) * dim] = dot(mixed, v_ref[:, at], 1, 0)


def across(half, dim, give, start, inners, have, last, place_ref, *refs):
    side = side_of(place_ref, give)
    q_ref, g_ref, gain_ref, cum_t_ref = refs[:4]
    inner = [ref[:, i * dim : (i + 1) * dim] for ref in refs[4 : 4 + inners] for i in range(ref.shape[1] // dim)]
    before = refs[4 + inners : 4 + inners + have]
    states = refs[4 + inners + have : -2]
    attn_ref, sums_ref = refs[-2:]
    lead = jnp.exp(cum_t_ref[...])
    squares = cross = jnp.zeros((lead.shape[0], dim), f32)
    j = start
    for ref in states:
        for i in range(ref.shape[0]):
            at = lanes(side, half, j, dim)
            hi, lo = split(ref[i])
            q = q_ref[:, at]
            outer = (dot(q, hi, 1, 0) + dot(q, lo, 1, 0)) * column(lead, side, half, j)
            attn = inner[j] + outer
            attn_ref[:, (j - start) * dim : (j - start + 1) * dim] = attn
            scaled = g_ref[:, at].astype(f32) * gain_ref[:, at]
            squares += attn * attn
            cross += scaled * attn
            j += 1
    for ref in before:
        squares += ref[0]
        cross += ref[1]
    if last:
        sums_ref[0:1, :] = jnp.sum(squares.T, axis=0, keepdims=True)
        sums_ref[1:2, :] = jnp.sum(cross.T, axis=0, keepdims=True)
        sums_ref[2:, :] = jnp.zeros((sums_ref.shape[0] - 2, sums_ref.shape[1]), f32)
    else:
        sums_ref[0] = squares
        sums_ref[1] = cross


def gradient(half, dim, give, full_width, n_sums, n_attn, place_ref, *refs):
    side = side_of(place_ref, give)
    q_ref, g_ref, gain_ref, cum_t_ref = refs[:4]
    sums = refs[4 : 4 + n_sums]
    attns = refs[4 + n_sums : 4 + n_sums + n_attn]
    d_ref, gain_part_ref = refs[4 + n_sums + n_attn :][:2]
    outs = refs[4 + n_sums + n_attn + 2 :]
    total = sums[0][...]
    for ref in sums[1:]:
        total = total + ref[...]
    inv_row = lax.rsqrt(total[0:1] / full_width + epsilon)
    mean_row = inv_row * (total[1:2] / full_width)
    tok = inv_row.shape[1]
    inv = jnp.broadcast_to(inv_row, (tok, tok)).T
    mean = jnp.broadcast_to(mean_row, (tok, tok)).T
    lead = jnp.exp(cum_t_ref[...])
    kept = {}
    j = 0
    for ref in attns:
        for i in range(ref.shape[1] // dim):
            at = lanes(side, half, j, dim)
            normed = ref[:, i * dim : (i + 1) * dim] * inv
            g = g_ref[:, at].astype(f32)
            d = (inv * (g * gain_ref[:, at] - normed * mean)).astype(bf16)
            d_ref[:, j * dim : (j + 1) * dim] = d
            gain_part_ref[j : j + 1, :] = jnp.sum(g * normed, axis=0, keepdims=True)
            kept[j] = d
            j += 1
    state_into(outs, lambda j: q_ref[:, lanes(side, half, j, dim)], lambda j: kept[j], lead, side, half)


def local_grads(half, dim, give, start, place_ref, *refs):
    side = side_of(place_ref, give)
    q_ref, k_ref, v_ref, cum_t_ref, cum_r_ref, mixed_ref, d_ref = refs[:7]
    query_ref, kg_ref, vg_ref = refs[-3:]
    cum_t = cum_t_ref[...]
    lead = jnp.exp(cum_t)
    count = 0
    for ref in refs[7:-3]:
        for n in range(ref.shape[0]):
            j = start + count
            at = lanes(side, half, j, dim)
            to = slice(count * dim, (count + 1) * dim)
            d = d_ref[:, j * dim : (j + 1) * dim]
            graded = (dot(d, v_ref[:, at], 1, 1) * weights_of(cum_t, cum_r_ref, side, half, j)).astype(bf16)
            hi, lo = split(ref[n])
            outer = (dot(d, hi, 1, 1) + dot(d, lo, 1, 1)) * column(lead, side, half, j)
            query_ref[:, to] = (dot(graded, k_ref[:, at], 1, 0) + outer).astype(bf16)
            kg_ref[:, to] = dot(graded, q_ref[:, at], 0, 0)
            vg_ref[:, to] = dot(mixed_ref[count], d, 0, 0)
            count += 1


def final_grads(half, dim, parts, pieces, queries, skip, place_ref, *refs):
    k_ref, v_ref, cum_t_ref = refs[:3]
    refs = refs[3:]
    local = {}
    for (give, first), kg_ref, vg_ref in zip(pieces, refs[::2], refs[1::2]):
        for i in range(kg_ref.shape[1] // dim):
            local[give, first + i] = (kg_ref, vg_ref, slice(i * dim, (i + 1) * dim))
    refs = refs[2 * len(pieces) :]
    states, query_pieces = refs[: len(parts)], refs[len(parts) : len(parts) + len(queries)]
    outs = refs[len(parts) + len(queries) + skip :]
    key_ref, value_ref = outs[:2]
    key_buf, value_buf, sems = outs[-3:]
    cum_t = cum_t_ref[...]
    tail = jnp.exp(cum_t[cum_t.shape[0] - 1 :, :] - cum_t)
    copies = []

    def put(source, out, give, j):
        side = side_of(place_ref, give)
        target = pl.ds(pl.multiple_of((side * half + j) * dim, dim), source.shape[1])
        copies.append(pltpu.make_async_copy(source, out.at[:, target], sems.at[len(copies)]))
        copies[-1].start()

    for ref, (give, j) in zip(query_pieces, queries):
        put(ref, outs[2], give, j)
    at = 0
    for ref, (give, j) in zip(states, parts):
        side = side_of(place_ref, give)
        size = ref.shape[0] * dim
        for i in range(ref.shape[0]):
            here = lanes(side, half, j + i, dim)
            to = slice(at + i * dim, at + (i + 1) * dim)
            tail_col = column(tail, side, half, j + i)
            hi, lo = split(ref[i])
            v, k = v_ref[:, here], k_ref[:, here]
            kg_ref, vg_ref, part = local[give, j + i]
            key_buf[:, to] = (kg_ref[:, part] + (dot(v, hi, 1, 1) + dot(v, lo, 1, 1)) * tail_col).astype(bf16)
            value_buf[:, to] = (vg_ref[:, part] + (dot(k, hi, 1, 0) + dot(k, lo, 1, 0)) * tail_col).astype(bf16)
        put(key_buf.at[:, at : at + size], key_ref, give, j)
        put(value_buf.at[:, at : at + size], value_ref, give, j)
        at += size
    for copy in copies:
        copy.wait()


def carried(mine, theirs, total_mine, total_theirs, flags, n_seq, n_dp, reverse):
    pairs = n_seq // 2
    first = flags[2 if reverse else 1]
    base = 2 + pairs if reverse else 3
    swap = [(i, i ^ 1) for i in range(n_seq)]

    def hop(a):
        b = a + 1
        lo, hi = (pairs - 1 - a, pairs - 1 - b) if reverse else (a, b)
        perm = []
        for s in range(n_seq):
            for d in range(n_dp):
                if s // 2 == lo:
                    to = (s + 2 * (hi - lo)) * n_dp + d
                elif s // 2 == hi:
                    to = (s - 2 * (hi - lo)) * n_dp + d
                else:
                    to = s * n_dp + (d ^ 1)
                perm.append((s * n_dp + d, to))
        return perm

    received = [lax.ppermute(x, "seq", swap) for x in theirs]
    kept, sent = [], []
    at = 0
    cuts = []
    for x in mine:
        n = x.shape[0]
        cuts.append((total_mine[at : at + n, None, :], total_theirs[at : at + n, None, :]))
        at += n
    sums = []
    for x, r, (my_decay, their_decay) in zip(mine, received, cuts):
        sums.append(jnp.where(first > 0.5, their_decay, 1.0) * x + jnp.where(first > 0.5, 1.0, my_decay) * r)
    both = [a * b for a, b in cuts]
    inward = [None] * len(mine)
    outward = sums
    for a in range(pairs - 1):
        got = [lax.ppermute(x, ("seq", "dp"), hop(a)) for x in outward]
        here = flags[base + a]
        inward = [
            jnp.where(here > 0.5, g, 0.0 if e is None else e) for g, e in zip(got, inward)
        ]
        outward = []
        for total, decay, g in zip(sums, both, got):
            outward.append(total + decay * g)
    for x, r, e, (my_decay, their_decay) in zip(mine, received, inward, cuts):
        if e is None:
            e = jnp.zeros_like(x)
        if sent:
            x, sent[-1] = lax.optimization_barrier((x, sent[-1]))
        through = jnp.where(first > 0.5, my_decay, their_decay) * e + jnp.where(first > 0.5, x, r)
        kept.append(jnp.where(first > 0.5, e, through))
        sent.append(jnp.where(first > 0.5, through, e))
    return kept, [lax.ppermute(x, "seq", swap) for x in sent]


def chunk_count(heads):
    return min(4, heads // 2)


def on_device(n_seq, n_dp, queries, keys, values, output_gradient, log_decay, gain):
    tok, width = queries.shape
    heads = log_decay.shape[0]
    dim = width // heads
    half = heads // 2
    chunks = chunk_count(heads)
    sizes = [half // chunks + (1 if i < half % chunks else 0) for i in range(chunks)]
    full_width = width * n_dp
    place = lax.axis_index("seq")
    pairs = n_seq // 2
    place = place.astype(jnp.int32).reshape(1)
    rows = -(-(1 + 2 * pairs) // 8) * 8
    gain_row = gain.reshape(1, width)
    pair_flops = 2 * tok * dim * dim
    state = [((n, dim, dim), f32) for n in sizes]
    row_bytes = tok * half * dim

    cum_t, cum_r, total, flags, *give = call(
        functools.partial(first_states, half, dim, pairs),
        [((tok, heads), f32), ((heads, tok), f32), ((heads, dim), f32), ((rows, dim), f32)] + state,
        2 * half * pair_flops, 8 * row_bytes,
        in_hbm=(0, 1, 2),
        scratch=[
            pltpu.VMEM((tok, half * dim), bf16),
            pltpu.VMEM((tok, half * dim), bf16),
            pltpu.VMEM((heads, tok), f32),
            pltpu.SemaphoreType.DMA((1 + 2 * chunks,)),
        ],
    )(place, keys, values, log_decay)
    swap = [(i, i ^ 1) for i in range(n_seq)]
    other = lax.ppermute(total, "seq", swap)
    own_states = call(
        functools.partial(more_states, half, dim), state, 2 * half * pair_flops, 8 * row_bytes
    )(place, keys, values, cum_t)
    places = [sum(sizes[:c]) for c in range(chunks)]
    middle = (chunks + 1) // 2
    pieces = [
        (give_piece, run)
        for give_piece in (False, True)
        for run in (list(range(middle)), list(range(middle, chunks)))
        if run
    ]
    mixed, inner = [], {False: [], True: []}
    for is_give, run in pieces:
        count = sum(sizes[c] for c in run)
        mix, inn = call(
            functools.partial(within, half, dim, is_give, places[run[0]]),
            [((count, tok, tok), bf16), ((tok, count * dim), f32)],
            2 * count * pair_flops, 12 * tok * count * dim,
        )(place, queries, keys, values, cum_t, cum_r)
        mixed.append(mix)
        inner[is_give].append(inn)

    upper = flags[0] > 0.5
    total_mine = jnp.where(upper, total[half:], total[:half])
    total_theirs = jnp.where(upper, other[half:], other[:half])
    in_own, in_give = carried(own_states, give, total_mine, total_theirs, flags, n_seq, n_dp, False)

    def outer(is_give, states, start, before, last):
        count = sum(x.shape[0] for x in states)
        return call(
            functools.partial(across, half, dim, is_give, start, len(inner[is_give]), len(before), last),
            [((tok, count * dim), f32), ((8, tok), f32) if last else ((2, tok, dim), f32)],
            2 * count * pair_flops, 14 * tok * count * dim,
        )(place, queries, output_gradient, gain_row, cum_t, *inner[is_give], *before, *states)

    attn_own, part = outer(False, in_own, 0, [], False)
    early = sum(sizes[:-1])
    if early:
        attn_early, more = outer(True, in_give[:-1], 0, [part], False)
        attn_late, sums = outer(True, in_give[-1:], early, [more], True)
        attn_give = [attn_early, attn_late]
    else:
        attn_late, sums = outer(True, in_give, 0, [part], True)
        attn_give = [attn_late]

    if n_dp <= 4:
        all_sums = [sums] + [
            lax.ppermute(sums, "dp", [(i, i ^ m) for i in range(n_dp)]) for m in range(1, n_dp)
        ]
    else:
        all_sums = [lax.psum(sums, "dp")]

    def grads(is_give, attns):
        return call(
            functools.partial(gradient, half, dim, is_give, full_width, len(all_sums), len(attns)),
            [((tok, half * dim), bf16), ((half, dim), f32)] + state,
            2 * half * pair_flops, 14 * row_bytes,
        )(place, queries, output_gradient, gain_row, cum_t, *all_sums, *attns)

    d_give, gain_give, *back_give = grads(True, attn_give)
    d_own, gain_own, *back_own = grads(False, [attn_own])
    query_pieces, local = [], []
    for n, (is_give, run) in enumerate(pieces):
        count = sum(sizes[c] for c in run)
        states = [(in_give if is_give else in_own)[c] for c in run]
        query, key_part, value_part = call(
            functools.partial(local_grads, half, dim, is_give, places[run[0]]),
            [((tok, count * dim), bf16), ((tok, count * dim), f32), ((tok, count * dim), f32)],
            6 * count * pair_flops, 40 * tok * count * dim,
        )(place, queries, keys, values, cum_t, cum_r, mixed[n], d_give if is_give else d_own, *states)
        query_pieces.append(((is_give, places[run[0]]), query))
        local.append(((is_give, places[run[0]]), key_part, value_part))

    late_own, late_give = carried(back_own, back_give, total_mine, total_theirs, flags, n_seq, n_dp, True)

    gain_grad = jnp.concatenate(
        [jnp.where(upper, gain_give, gain_own), jnp.where(upper, gain_own, gain_give)], axis=0
    )
    step = 1
    while step < n_seq:
        moved = lax.ppermute(gain_grad, "seq", [(i, i ^ step) for i in range(n_seq)])
        gain_grad = gain_grad + moved
        if 2 * step >= n_seq:
            gain_grad = gain_grad.reshape(width)
        step *= 2

    def finish(parts, states, query_parts, before):
        count = sum(x.shape[0] for x in states)
        used = [
            (mark, key_part, value_part)
            for mark, key_part, value_part in local
            if any(mark[0] == g and mark[1] <= p < mark[1] + key_part.shape[1] // dim for g, p in parts)
        ]
        base = 3 + 2 * len(used) + len(parts) + len(query_parts)
        outs = 3 if query_parts else 2
        return call(
            functools.partial(
                final_grads, half, dim, parts, [u[0] for u in used], [q for q, _ in query_parts], len(before)
            ),
            [((tok, width), bf16)] * outs,
            4 * count * pair_flops, 20 * tok * count * dim,
            in_hbm=(base, base + 1),
            outs_in_hbm=range(outs),
            scratch=[
                pltpu.VMEM((tok, count * dim), bf16),
                pltpu.VMEM((tok, count * dim), bf16),
                pltpu.SemaphoreType.DMA((2 * len(parts) + len(query_parts),)),
            ],
            aliases={base + 1: 0, base + 2: 1} if before else None,
        )(
            place, keys, values, cum_t, *[x for _, a, b in used for x in (a, b)], *states,
            *[q for _, q in query_parts], *before,
        )

    own_parts = [(False, p) for p in places]
    give_parts = [(True, p) for p in places]
    begun = finish(own_parts, late_own, [], [])
    if chunks > 1:
        *begun, query_grad = finish(give_parts[:-1], late_give[:-1], query_pieces, begun)
        key_grad, value_grad = finish(give_parts[-1:], late_give[-1:], [], begun)
    else:
        key_grad, value_grad, query_grad = finish(give_parts, late_give, query_pieces, begun)
    return query_grad, key_grad, value_grad, gain_grad


def solution(mesh):
    n_seq, n_dp = mesh.shape["seq"], mesh.shape["dp"]

    def body(*args):
        return on_device(n_seq, n_dp, *args)

    return jax.shard_map(
        body,
        mesh=mesh,
        in_specs=(P("seq", "dp"), P("seq", "dp"), P("seq", "dp"), P("seq", "dp"), P("dp", "seq"), P("dp")),
        out_specs=(P("seq", "dp"), P("seq", "dp"), P("seq", "dp"), P("dp")),
        check_vma=False,
    )
```

```python
import functools

import jax
import jax.numpy as jnp
from jax import lax
from jax.experimental import pallas as pl
from jax.experimental.pallas import tpu as pltpu
from jax.sharding import PartitionSpec as P


epsilon = 1e-05
highest = lax.Precision.HIGHEST
f32 = jnp.float32
bf16 = jnp.bfloat16
VMEM = pl.BlockSpec(memory_space=pltpu.VMEM)
SMEM = pl.BlockSpec(memory_space=pltpu.SMEM)
HBM = pl.BlockSpec(memory_space=pltpu.HBM)
GRANT = 24 * 2**20


def call(body, outs, flops, moved, in_hbm=(), outs_in_hbm=(), scratch=(), aliases=None):
    def run(place, *arrays):
        arrays = [pltpu.with_memory_space_constraint(x, pltpu.HBM) if i in in_hbm and not aliases else x for i, x in enumerate(arrays)]
        return pl.pallas_call(
            body,
            out_shape=[jax.ShapeDtypeStruct(*o) for o in outs],
            in_specs=[SMEM] + [HBM if i in in_hbm else VMEM for i in range(len(arrays))],
            out_specs=[HBM if i in outs_in_hbm else VMEM for i in range(len(outs))],
            scratch_shapes=list(scratch),
            input_output_aliases=aliases or {},
            compiler_params=pltpu.CompilerParams(vmem_limit_bytes=GRANT),
            cost_estimate=pl.CostEstimate(flops=flops, bytes_accessed=moved, transcendentals=0),
        )(place, *arrays)

    return run


def dot(a, b, ca, cb):
    return lax.dot_general(a, b, (((ca,), (cb,)), ((), ())), preferred_element_type=f32)


def split(x):
    hi = x.astype(bf16)
    return hi, (x - hi.astype(f32)).astype(bf16)


def column(table, side, half, j):
    return jnp.where(side == 0, table[:, j : j + 1], table[:, half + j : half + j + 1])


def side_of(place_ref, give):
    own = place_ref[0] & 1
    return 1 - own if give else own


def flags_of(place, pairs, shape):
    row = lax.broadcasted_iota(jnp.int32, shape, 0)
    odd, pair = place & 1, place >> 1
    forward = (row >= 3) & (row < 2 + pairs) & (row - 2 == pair)
    reverse = (row >= 2 + pairs) & (row < 1 + 2 * pairs) & (row - 1 - pairs == pairs - 1 - pair)
    even = jnp.full(shape, odd, jnp.int32) == 0
    on = ((row == 0) & ~even) | ((row == 1) & even) | ((row == 2) & ~even) | forward | reverse
    return on.astype(f32)


def lanes(side, half, j, dim):
    return pl.ds(pl.multiple_of((side * half + j) * dim, dim), dim)


def tables(ld):
    tok = ld.shape[1]
    row = lax.broadcasted_iota(jnp.int32, (tok, tok), 0)
    col = lax.broadcasted_iota(jnp.int32, (tok, tok), 1)
    lower = (row >= col).astype(f32)
    dims = (((1,), (1,)), ((), ()))
    cum_t = lax.dot_general(lower, ld, dims, precision=highest, preferred_element_type=f32)
    cum_r = lax.dot_general(ld, lower, dims, precision=highest, preferred_element_type=f32)
    return cum_t, cum_r


def state_into(outs, a_of, b_of, factor, side, half, start=0):
    j = start
    for out in outs:
        for i in range(out.shape[0]):
            hi, lo = split(a_of(j).astype(f32) * column(factor, side, half, j))
            b = b_of(j)
            out[i] = dot(hi, b, 0, 0) + dot(lo, b, 0, 0)
            j += 1


def first_states(half, dim, pairs, place_ref, k_ref, v_ref, ld_ref, cum_t_ref, cum_r_ref, total_ref, flags_ref, *refs):
    outs, (k_buf, v_buf, ld_buf, sems) = refs[:-4], refs[-4:]
    side = side_of(place_ref, True)
    copies = [pltpu.make_async_copy(ld_ref, ld_buf, sems.at[0])]
    at = 0
    for c, out in enumerate(outs):
        size = out.shape[0] * dim
        source = pl.ds(pl.multiple_of((side * half) * dim + at, dim), size)
        for n, (ref, buf) in enumerate(((k_ref, k_buf), (v_ref, v_buf))):
            copies.append(pltpu.make_async_copy(ref.at[:, source], buf.at[:, at : at + size], sems.at[1 + 2 * c + n]))
        at += size
    for copy in copies:
        copy.start()
    flags_ref[...] = flags_of(place_ref[0], pairs, flags_ref.shape)
    copies[0].wait()
    cum_t, cum_r = tables(ld_buf[...])
    cum_t_ref[...] = cum_t
    cum_r_ref[...] = cum_r
    tok = cum_t.shape[0]
    total_ref[...] = jnp.broadcast_to(jnp.exp(cum_r[:, tok - 1 :]), total_ref.shape)
    tail = jnp.exp(cum_t[tok - 1 :, :] - cum_t)
    start = 0
    for c, out in enumerate(outs):
        copies[1 + 2 * c].wait()
        copies[2 + 2 * c].wait()
        state_into(
            [out],
            lambda j: k_buf[:, j * dim : (j + 1) * dim],
            lambda j: v_buf[:, j * dim : (j + 1) * dim],
            tail, side, half, start,
        )
        start += out.shape[0]


def more_states(half, dim, give, start, place_ref, k_ref, v_ref, cum_t_ref, *outs):
    side = side_of(place_ref, give)
    cum_t = cum_t_ref[...]
    tail = jnp.exp(cum_t[cum_t.shape[0] - 1 :, :] - cum_t)
    state_into(
        outs,
        lambda j: k_ref[:, lanes(side, half, j, dim)],
        lambda j: v_ref[:, lanes(side, half, j, dim)],
        tail, side, half, start,
    )


def weights_of(cum_t, cum_r_ref, side, half, j):
    tok = cum_t.shape[0]
    row = lax.broadcasted_iota(jnp.int32, (tok, tok), 0)
    col = lax.broadcasted_iota(jnp.int32, (tok, tok), 1)
    gap = column(cum_t, side, half, j) - cum_r_ref[pl.ds(side * half + j, 1), :]
    return jnp.where(row >= col, jnp.exp(jnp.minimum(gap, 0.0)), 0.0)


def within(half, dim, give, start, place_ref, q_ref, k_ref, v_ref, cum_t_ref, cum_r_ref, mixed_ref, inner_ref):
    side = side_of(place_ref, give)
    cum_t = cum_t_ref[...]
    for i in range(mixed_ref.shape[0]):
        at = lanes(side, half, start + i, dim)
        scores = dot(q_ref[:, at], k_ref[:, at], 1, 1)
        mixed = (scores * weights_of(cum_t, cum_r_ref, side, half, start + i)).astype(bf16)
        mixed_ref[i] = mixed
        inner_ref[:, i * dim : (i + 1) * dim] = dot(mixed, v_ref[:, at], 1, 0)


def across(half, dim, give, start, inners, have, last, place_ref, *refs):
    side = side_of(place_ref, give)
    q_ref, g_ref, gain_ref, cum_t_ref = refs[:4]
    inner = [ref[:, i * dim : (i + 1) * dim] for ref in refs[4 : 4 + inners] for i in range(ref.shape[1] // dim)]
    before = refs[4 + inners : 4 + inners + have]
    states = refs[4 + inners + have : -2]
    attn_ref, sums_ref = refs[-2:]
    lead = jnp.exp(cum_t_ref[...])
    squares = cross = jnp.zeros((lead.shape[0], dim), f32)
    j = start
    for ref in states:
        for i in range(ref.shape[0]):
            at = lanes(side, half, j, dim)
            hi, lo = split(ref[i])
            q = q_ref[:, at]
            outer = (dot(q, hi, 1, 0) + dot(q, lo, 1, 0)) * column(lead, side, half, j)
            attn = inner[j] + outer
            attn_ref[:, (j - start) * dim : (j - start + 1) * dim] = attn
            scaled = g_ref[:, at].astype(f32) * gain_ref[:, at]
            squares += attn * attn
            cross += scaled * attn
            j += 1
    for ref in before:
        squares += ref[0]
        cross += ref[1]
    if last:
        sums_ref[0:1, :] = jnp.sum(squares.T, axis=0, keepdims=True)
        sums_ref[1:2, :] = jnp.sum(cross.T, axis=0, keepdims=True)
        sums_ref[2:, :] = jnp.zeros((sums_ref.shape[0] - 2, sums_ref.shape[1]), f32)
    else:
        sums_ref[0] = squares
        sums_ref[1] = cross


def gradient(half, dim, give, start, full_width, n_sums, n_attn, place_ref, *refs):
    side = side_of(place_ref, give)
    q_ref, g_ref, gain_ref, cum_t_ref = refs[:4]
    sums = refs[4 : 4 + n_sums]
    attns = refs[4 + n_sums : 4 + n_sums + n_attn]
    d_ref, gain_part_ref = refs[4 + n_sums + n_attn :][:2]
    outs = refs[4 + n_sums + n_attn + 2 :]
    total = sums[0][...]
    for ref in sums[1:]:
        total = total + ref[...]
    inv_row = lax.rsqrt(total[0:1] / full_width + epsilon)
    mean_row = inv_row * (total[1:2] / full_width)
    tok = inv_row.shape[1]
    inv = jnp.broadcast_to(inv_row, (tok, tok)).T
    mean = jnp.broadcast_to(mean_row, (tok, tok)).T
    lead = jnp.exp(cum_t_ref[...])
    attn = [ref[:, i * dim : (i + 1) * dim] for ref in attns for i in range(ref.shape[1] // dim)]
    kept = {}
    for i in range(d_ref.shape[1] // dim):
        j = start + i
        at = lanes(side, half, j, dim)
        normed = attn[j] * inv
        g = g_ref[:, at].astype(f32)
        d = (inv * (g * gain_ref[:, at] - normed * mean)).astype(bf16)
        d_ref[:, i * dim : (i + 1) * dim] = d
        gain_part_ref[i : i + 1, :] = jnp.sum(g * normed, axis=0, keepdims=True)
        kept[j] = d
    state_into(outs, lambda j: q_ref[:, lanes(side, half, j, dim)], lambda j: kept[j], lead, side, half, start)


def local_grads(half, dim, give, start, n_d, place_ref, *refs):
    side = side_of(place_ref, give)
    q_ref, k_ref, v_ref, cum_t_ref, cum_r_ref, mixed_ref = refs[:6]
    d_all = [ref[:, i * dim : (i + 1) * dim] for ref in refs[6 : 6 + n_d] for i in range(ref.shape[1] // dim)]
    query_ref, kg_ref, vg_ref = refs[-3:]
    cum_t = cum_t_ref[...]
    lead = jnp.exp(cum_t)
    count = 0
    for ref in refs[6 + n_d : -3]:
        for n in range(ref.shape[0]):
            j = start + count
            at = lanes(side, half, j, dim)
            to = slice(count * dim, (count + 1) * dim)
            d = d_all[j]
            graded = (dot(d, v_ref[:, at], 1, 1) * weights_of(cum_t, cum_r_ref, side, half, j)).astype(bf16)
            hi, lo = split(ref[n])
            outer = (dot(d, hi, 1, 1) + dot(d, lo, 1, 1)) * column(lead, side, half, j)
            query_ref[:, to] = (dot(graded, k_ref[:, at], 1, 0) + outer).astype(bf16)
            kg_ref[:, to] = dot(graded, q_ref[:, at], 0, 0)
            vg_ref[:, to] = dot(mixed_ref[count], d, 0, 0)
            count += 1


def final_grads(half, dim, parts, pieces, queries, skip, place_ref, *refs):
    k_ref, v_ref, cum_t_ref = refs[:3]
    refs = refs[3:]
    local = {}
    for (give, first), kg_ref, vg_ref in zip(pieces, refs[::2], refs[1::2]):
        for i in range(kg_ref.shape[1] // dim):
            local[give, first + i] = (kg_ref, vg_ref, slice(i * dim, (i + 1) * dim))
    refs = refs[2 * len(pieces) :]
    states, query_pieces = refs[: len(parts)], refs[len(parts) : len(parts) + len(queries)]
    outs = refs[len(parts) + len(queries) + skip :]
    key_ref, value_ref = outs[:2]
    key_buf, value_buf, sems = outs[-3:]
    cum_t = cum_t_ref[...]
    tail = jnp.exp(cum_t[cum_t.shape[0] - 1 :, :] - cum_t)
    copies = []

    def put(source, out, give, j):
        side = side_of(place_ref, give)
        target = pl.ds(pl.multiple_of((side * half + j) * dim, dim), source.shape[1])
        copies.append(pltpu.make_async_copy(source, out.at[:, target], sems.at[len(copies)]))
        copies[-1].start()

    for ref, (give, j) in zip(query_pieces, queries):
        put(ref, outs[2], give, j)
    at = 0
    for ref, (give, j) in zip(states, parts):
        side = side_of(place_ref, give)
        size = ref.shape[0] * dim
        for i in range(ref.shape[0]):
            here = lanes(side, half, j + i, dim)
            to = slice(at + i * dim, at + (i + 1) * dim)
            tail_col = column(tail, side, half, j + i)
            hi, lo = split(ref[i])
            v, k = v_ref[:, here], k_ref[:, here]
            kg_ref, vg_ref, part = local[give, j + i]
            key_buf[:, to] = (kg_ref[:, part] + (dot(v, hi, 1, 1) + dot(v, lo, 1, 1)) * tail_col).astype(bf16)
            value_buf[:, to] = (vg_ref[:, part] + (dot(k, hi, 1, 0) + dot(k, lo, 1, 0)) * tail_col).astype(bf16)
        put(key_buf.at[:, at : at + size], key_ref, give, j)
        put(value_buf.at[:, at : at + size], value_ref, give, j)
        at += size
    for copy in copies:
        copy.wait()


def carried(mine, theirs, total_mine, total_theirs, flags, n_seq, n_dp, reverse):
    pairs = n_seq // 2
    first = flags[2 if reverse else 1]
    base = 2 + pairs if reverse else 3
    swap = [(i, i ^ 1) for i in range(n_seq)]

    def hop(a):
        b = a + 1
        lo, hi = (pairs - 1 - a, pairs - 1 - b) if reverse else (a, b)
        perm = []
        for s in range(n_seq):
            for d in range(n_dp):
                if s // 2 == lo:
                    to = (s + 2 * (hi - lo)) * n_dp + d
                elif s // 2 == hi:
                    to = (s - 2 * (hi - lo)) * n_dp + d
                else:
                    to = s * n_dp + (d ^ 1)
                perm.append((s * n_dp + d, to))
        return perm

    received = [lax.ppermute(x, "seq", swap) for x in theirs]
    kept, sent = [], []
    at = 0
    cuts = []
    for x in mine:
        n = x.shape[0]
        cuts.append((total_mine[at : at + n, None, :], total_theirs[at : at + n, None, :]))
        at += n
    sums = []
    for x, r, (my_decay, their_decay) in zip(mine, received, cuts):
        sums.append(jnp.where(first > 0.5, their_decay, 1.0) * x + jnp.where(first > 0.5, 1.0, my_decay) * r)
    both = [a * b for a, b in cuts]
    inward = [None] * len(mine)
    outward = sums
    for a in range(pairs - 1):
        got = [lax.ppermute(x, ("seq", "dp"), hop(a)) for x in outward]
        here = flags[base + a]
        inward = [
            jnp.where(here > 0.5, g, 0.0 if e is None else e) for g, e in zip(got, inward)
        ]
        outward = []
        for total, decay, g in zip(sums, both, got):
            outward.append(total + decay * g)
    for x, r, e, (my_decay, their_decay) in zip(mine, received, inward, cuts):
        if e is None:
            e = jnp.zeros_like(x)
        if sent:
            x, sent[-1] = lax.optimization_barrier((x, sent[-1]))
        through = jnp.where(first > 0.5, my_decay, their_decay) * e + jnp.where(first > 0.5, x, r)
        kept.append(jnp.where(first > 0.5, e, through))
        sent.append(jnp.where(first > 0.5, through, e))
    return kept, [lax.ppermute(x, "seq", swap) for x in sent]


def chunk_count(heads):
    return min(4, heads // 2)


def on_device(n_seq, n_dp, queries, keys, values, output_gradient, log_decay, gain):
    tok, width = queries.shape
    heads = log_decay.shape[0]
    dim = width // heads
    half = heads // 2
    chunks = chunk_count(heads)
    sizes = [half // chunks + (1 if i < half % chunks else 0) for i in range(chunks)]
    full_width = width * n_dp
    place = lax.axis_index("seq")
    pairs = n_seq // 2
    place = place.astype(jnp.int32).reshape(1)
    rows = -(-(1 + 2 * pairs) // 8) * 8
    gain_row = gain.reshape(1, width)
    pair_flops = 2 * tok * dim * dim
    state = [((n, dim, dim), f32) for n in sizes]
    row_bytes = tok * half * dim

    first = sizes[0]
    cum_t, cum_r, total, flags, *give = call(
        functools.partial(first_states, half, dim, pairs),
        [((tok, heads), f32), ((heads, tok), f32), ((heads, dim), f32), ((rows, dim), f32)] + state[:1],
        2 * first * pair_flops, 8 * tok * first * dim,
        in_hbm=(0, 1, 2),
        scratch=[
            pltpu.VMEM((tok, first * dim), bf16),
            pltpu.VMEM((tok, first * dim), bf16),
            pltpu.VMEM((heads, tok), f32),
            pltpu.SemaphoreType.DMA((3,)),
        ],
    )(place, keys, values, log_decay)

    def states_of(is_give, start, outs):
        return call(
            functools.partial(more_states, half, dim, is_give, start),
            outs, 2 * half * pair_flops, 8 * row_bytes,
        )(place, keys, values, cum_t)

    if chunks > 1:
        give += states_of(True, first, state[1:])
    swap = [(i, i ^ 1) for i in range(n_seq)]
    other = lax.ppermute(total, "seq", swap)
    own_states = states_of(False, 0, state)
    places = [sum(sizes[:c]) for c in range(chunks)]
    middle = (chunks + 1) // 2
    pieces = [
        (give_piece, run)
        for give_piece in (False, True)
        for run in (list(range(middle)), list(range(middle, chunks)))
        if run
    ]
    mixed, inner = [], {False: [], True: []}
    for is_give, run in pieces:
        count = sum(sizes[c] for c in run)
        mix, inn = call(
            functools.partial(within, half, dim, is_give, places[run[0]]),
            [((count, tok, tok), bf16), ((tok, count * dim), f32)],
            2 * count * pair_flops, 12 * tok * count * dim,
        )(place, queries, keys, values, cum_t, cum_r)
        mixed.append(mix)
        inner[is_give].append(inn)

    upper = flags[0] > 0.5
    total_mine = jnp.where(upper, total[half:], total[:half])
    total_theirs = jnp.where(upper, other[half:], other[:half])
    in_own, in_give = carried(own_states, give, total_mine, total_theirs, flags, n_seq, n_dp, False)

    def outer(is_give, states, start, before, last):
        count = sum(x.shape[0] for x in states)
        return call(
            functools.partial(across, half, dim, is_give, start, len(inner[is_give]), len(before), last),
            [((tok, count * dim), f32), ((8, tok), f32) if last else ((2, tok, dim), f32)],
            2 * count * pair_flops, 14 * tok * count * dim,
        )(place, queries, output_gradient, gain_row, cum_t, *inner[is_give], *before, *states)

    attn_own, part = outer(False, in_own, 0, [], False)
    early = sum(sizes[:-1])
    if early:
        attn_early, more = outer(True, in_give[:-1], 0, [part], False)
        attn_late, sums = outer(True, in_give[-1:], early, [more], True)
        attn_give = [attn_early, attn_late]
    else:
        attn_late, sums = outer(True, in_give, 0, [part], True)
        attn_give = [attn_late]

    if n_dp <= 4:
        all_sums = [sums] + [
            lax.ppermute(sums, "dp", [(i, i ^ m) for i in range(n_dp)]) for m in range(1, n_dp)
        ]
    else:
        all_sums = [lax.psum(sums, "dp")]

    def grads(is_give, attns, run):
        count = sum(sizes[c] for c in run)
        return call(
            functools.partial(
                gradient, half, dim, is_give, places[run[0]], full_width, len(all_sums), len(attns)
            ),
            [((tok, count * dim), bf16), ((count, dim), f32)] + [state[c] for c in run],
            2 * count * pair_flops, 14 * tok * count * dim,
        )(place, queries, output_gradient, gain_row, cum_t, *all_sums, *attns)

    d_first, gain_first, *back_give = grads(True, attn_give, [0])
    d_give, gain_give = [d_first], [gain_first]
    if chunks > 1:
        d_rest, gain_rest, *back_rest = grads(True, attn_give, list(range(1, chunks)))
        d_give.append(d_rest)
        gain_give.append(gain_rest)
        back_give += back_rest
    gain_give = jnp.concatenate(gain_give, axis=0)
    d_own, gain_own, *back_own = grads(False, [attn_own], list(range(chunks)))
    d_own = [d_own]
    query_pieces, local = [], []
    for n, (is_give, run) in enumerate(pieces):
        count = sum(sizes[c] for c in run)
        states = [(in_give if is_give else in_own)[c] for c in run]
        d_side = d_give if is_give else d_own
        query, key_part, value_part = call(
            functools.partial(local_grads, half, dim, is_give, places[run[0]], len(d_side)),
            [((tok, count * dim), bf16), ((tok, count * dim), f32), ((tok, count * dim), f32)],
            6 * count * pair_flops, 40 * tok * count * dim,
        )(place, queries, keys, values, cum_t, cum_r, mixed[n], *d_side, *states)
        query_pieces.append(((is_give, places[run[0]]), query))
        local.append(((is_give, places[run[0]]), key_part, value_part))

    late_own, late_give = carried(back_own, back_give, total_mine, total_theirs, flags, n_seq, n_dp, True)

    gain_grad = jnp.concatenate(
        [jnp.where(upper, gain_give, gain_own), jnp.where(upper, gain_own, gain_give)], axis=0
    )
    step = 1
    while step < n_seq:
        moved = lax.ppermute(gain_grad, "seq", [(i, i ^ step) for i in range(n_seq)])
        gain_grad = gain_grad + moved
        if 2 * step >= n_seq:
            gain_grad = gain_grad.reshape(width)
        step *= 2

    def finish(parts, states, query_parts, before):
        count = sum(x.shape[0] for x in states)
        used = [
            (mark, key_part, value_part)
            for mark, key_part, value_part in local
            if any(mark[0] == g and mark[1] <= p < mark[1] + key_part.shape[1] // dim for g, p in parts)
        ]
        base = 3 + 2 * len(used) + len(parts) + len(query_parts)
        outs = 3 if query_parts else 2
        return call(
            functools.partial(
                final_grads, half, dim, parts, [u[0] for u in used], [q for q, _ in query_parts], len(before)
            ),
            [((tok, width), bf16)] * outs,
            4 * count * pair_flops, 20 * tok * count * dim,
            in_hbm=(base, base + 1),
            outs_in_hbm=range(outs),
            scratch=[
                pltpu.VMEM((tok, count * dim), bf16),
                pltpu.VMEM((tok, count * dim), bf16),
                pltpu.SemaphoreType.DMA((2 * len(parts) + len(query_parts),)),
            ],
            aliases={base + 1: 0, base + 2: 1} if before else None,
        )(
            place, keys, values, cum_t, *[x for _, a, b in used for x in (a, b)], *states,
            *[q for _, q in query_parts], *before,
        )

    own_parts = [(False, p) for p in places]
    give_parts = [(True, p) for p in places]
    begun = finish(own_parts, late_own, [], [])
    if chunks > 1:
        *begun, query_grad = finish(give_parts[:-1], late_give[:-1], query_pieces, begun)
        key_grad, value_grad = finish(give_parts[-1:], late_give[-1:], [], begun)
    else:
        key_grad, value_grad, query_grad = finish(give_parts, late_give, query_pieces, begun)
    return query_grad, key_grad, value_grad, gain_grad


def solution(mesh):
    n_seq, n_dp = mesh.shape["seq"], mesh.shape["dp"]

    def body(*args):
        return on_device(n_seq, n_dp, *args)

    return jax.shard_map(
        body,
        mesh=mesh,
        in_specs=(P("seq", "dp"), P("seq", "dp"), P("seq", "dp"), P("seq", "dp"), P("dp", "seq"), P("dp")),
        out_specs=(P("seq", "dp"), P("seq", "dp"), P("seq", "dp"), P("dp")),
        check_vma=False,
    )
```
